128 devices in a mesh: seq: 32 (over z, y, core), tp: 4 (over x).
Axes of the slice: x: 4, y: 4, z: 4, core: 2. Of those that a mesh axis runs over, the one named last changes fastest.
Arguments:
- states: bfloat16 [256, 3072], P(None, 'seq'), may hold values from -20 to 20
- norm_gain: bfloat16 [3072], P('seq'), may hold values from 0.25 to 1.75
- w_qkv: bfloat16 [3, 3072, 3072], P(None, 'seq', 'tp'), may hold values from -0.109375 to 0.109375
- w_out: bfloat16 [3072, 3072], P('tp', 'seq'), may hold values from -0.109375 to 0.109375
- cache: bfloat16 [768, 2, 64, 3072], P('seq', None, None, 'tp'), may hold values from -400 to 400
- context_len: int32 [256], replicated, may hold values from 1 to 4096, as said below
- block_owner: int32 [768], P('seq'), may hold values from 0 to 256, as said below
- block_index: int32 [768], P('seq'), may hold values from 0 to 63, as said below
Outputs:
- hidden: bfloat16 [256, 3072], P('tp', 'seq')
- updated: bfloat16 [768, 2, 64, 3072], P('seq', None, None, 'tp')
The draws below stay inside these ranges and needn't reach their ends.
Inputs may be any that keep to these rules, and one draw needn't show every extreme that they name: `context_len`: A request of length n owns exactly ceil(n / 64) pool blocks, with block_index 0, 1, ... once each; at least one pool block is unused. `context_len`: exactly 4 requests own 64/2 blocks or more; every other request owns at most 2 blocks, all on one index of seq. `block_owner`: the value 256 marks an unused block. `block_index`: 0 for an unused block.
All inputs are finite; a program needn't handle non-finite values.
Results may differ from the reference program's by a relative error of at most 0.0068.
Values may be sent and summed in bfloat16 or wider, within the bound.
A program may use at most 128 MiB of HBM per device.

```python
import jax
import jax.numpy as jnp
from jax import lax

D = 3072
HEAD_DIM = 96
BLOCK_TOKENS = 64
MAX_BLOCKS = 64
REQS = 256
BLOCKS_DEV = 24
POOL = 768
LONG_REQS = 4
ATT_WIDTH = 3072
N_SEQ = 32


def layout(key):
    base_key = jax.random.fold_in(key, 11)
    split_keys = jax.random.split(base_key, 5)
    order = jax.random.permutation(split_keys[0], REQS)
    ranks = jnp.argsort(order).astype(jnp.int32)
    short_rank = ranks - LONG_REQS
    short_count = jax.random.randint(split_keys[1], (REQS,), 1, 3)
    long_count = jax.random.randint(split_keys[2], (REQS,), MAX_BLOCKS // 2, MAX_BLOCKS + 1)
    counts = jnp.where(ranks == 0, MAX_BLOCKS, jnp.where(ranks < LONG_REQS, long_count, jnp.where(short_rank == 0, 1, short_count))).astype(jnp.int32)
    tails = jax.random.randint(split_keys[3], (REQS,), 1, BLOCK_TOKENS + 1)
    lengths = jnp.where(ranks == 0, MAX_BLOCKS * BLOCK_TOKENS, (counts - 1) * BLOCK_TOKENS + tails).astype(jnp.int32)
    place_j = jnp.arange(MAX_BLOCKS, dtype=jnp.int32)
    used = place_j[None, :] < counts[:, None]
    long_device = (ranks[:, None] * MAX_BLOCKS + place_j[None, :]) % N_SEQ
    short_device = jnp.broadcast_to((jnp.maximum(short_rank, 0) % N_SEQ)[:, None], (REQS, MAX_BLOCKS))
    device = jnp.where(ranks[:, None] < LONG_REQS, long_device, short_device).astype(jnp.int32).reshape(-1)
    used_flat = used.reshape(-1)
    onehot = ((device[:, None] == jnp.arange(N_SEQ, dtype=jnp.int32)[None, :]) & used_flat[:, None]).astype(jnp.int32)
    before = jnp.cumsum(onehot, axis=0).astype(jnp.int32) - onehot
    local = jnp.take_along_axis(before, device[:, None], axis=1)[:, 0]
    perms = jax.vmap(lambda sub_key: jax.random.permutation(sub_key, BLOCKS_DEV))(jax.random.split(split_keys[4], N_SEQ)).astype(jnp.int32)
    slot_place = device * BLOCKS_DEV + perms[device, jnp.minimum(local, BLOCKS_DEV - 1)]
    position = jnp.where(used_flat, slot_place, POOL).astype(jnp.int32)
    owners = jnp.repeat(jnp.arange(REQS, dtype=jnp.int32), MAX_BLOCKS)
    indices = jnp.tile(place_j, REQS)
    owner_table = jnp.full((POOL,), REQS, jnp.int32).at[position].set(owners, mode='drop')
    index_table = jnp.zeros((POOL,), jnp.int32).at[position].set(indices, mode='drop')
    return (lengths, owner_table, index_table)


def draw_context_len(key, part):
    return layout(key)[0]


def draw_block_owner(key, part):
    return layout(key)[1]


def draw_block_index(key, part):
    return layout(key)[2]


def draw_states(key, part):
    split_keys = jax.random.split(jax.random.fold_in(key, 23), 2)
    column_scale = 3.0 ** (jnp.arange(D, dtype=jnp.float32) / D) * jax.random.uniform(split_keys[1], (1, D), jnp.float32, 0.5, 1.5)
    base = jnp.clip(jax.random.normal(split_keys[0], (REQS, D), jnp.float32), -6.0, 6.0)
    values = 0.25 * base * column_scale
    return values.astype(jnp.bfloat16)


def draw_cache(key, part):
    split_keys = jax.random.split(jax.random.fold_in(key, 37), 1)
    base = jnp.clip(jax.random.normal(split_keys[0], (POOL, 2, BLOCK_TOKENS, ATT_WIDTH), jnp.float32), -6.0, 6.0)
    return base.astype(jnp.bfloat16)


def level_of(rng, dims, pieces, low, high):
    loudness = 1.0
    for dim, parts in pieces:
        steps = jax.random.uniform(jax.random.fold_in(jax.random.fold_in(rng, 6), dim), (parts,), jnp.float32, low / len(pieces), high / len(pieces))
        loudness = loudness * jnp.repeat(jnp.exp(steps), dims[dim] // parts).reshape((-1,) + (1,) * (len(dims) - 1 - dim))
    return loudness


def noise(own_key, shape, scale, reach, cuts=(), kind=jnp.bfloat16):
    gain = level_of(own_key, shape, cuts, -0.22, 0.18) if cuts else 1.0
    drawn = jax.random.normal(own_key, shape, jnp.float32) * scale * gain
    return jnp.minimum(jnp.maximum(drawn, -reach), reach).astype(kind)


def setup_inputs(seed: int = 0) -> dict:
    splits = jax.random.split(jax.random.key(seed), 9)
    return {
        "states": draw_states(jax.random.fold_in(splits[8], 71), 0),
        "norm_gain": jnp.clip(1.0 + 0.15 * jax.random.normal(splits[1], (D,), jnp.float32), 0.25, 1.75).astype(jnp.bfloat16),
        "w_qkv": noise(splits[2], (3, D, ATT_WIDTH), D ** -0.5, 0.109375, ((1, 32), (2, 4))),
        "w_out": noise(splits[3], (ATT_WIDTH, D), ATT_WIDTH ** -0.5, 0.109375, ((0, 4), (1, 32))),
        "cache": draw_cache(jax.random.fold_in(splits[8], 71), 0),
        "context_len": draw_context_len(jax.random.fold_in(splits[8], 71), 0),
        "block_owner": draw_block_owner(jax.random.fold_in(splits[8], 71), 0),
        "block_index": draw_block_index(jax.random.fold_in(splits[8], 71), 0),
    }


EPSILON = 1e-05
NEG_FLOOR = -1e+30

def rotate(values, positions):
    half_dim = HEAD_DIM // 2
    frequency = 10000.0 ** (-jnp.arange(half_dim, dtype=jnp.float32) * 2.0 / HEAD_DIM)
    angles = positions.astype(jnp.float32)[:, None] * frequency[None, :]
    cosine = jnp.cos(angles)[:, None, :]
    sine_part = jnp.sin(angles)[:, None, :]
    front_half = values[..., :half_dim]
    back_half = values[..., half_dim:]
    return jnp.concatenate([front_half * cosine - back_half * sine_part, back_half * cosine + front_half * sine_part], axis=-1)

def finish(projected, positions):
    row_count = projected.shape[0]
    columns = projected.shape[2]
    head_count = columns // HEAD_DIM
    query = rotate(projected[:, 0].reshape(row_count, head_count, HEAD_DIM), positions) * HEAD_DIM ** (-0.5)
    keys_new = rotate(projected[:, 1].reshape(row_count, head_count, HEAD_DIM), positions)
    return (query.astype(jnp.bfloat16).reshape(row_count, columns), keys_new.astype(jnp.bfloat16).reshape(row_count, columns), projected[:, 2].astype(jnp.bfloat16))

def append(cache, keys_new, values_new, context_len, block_owner, block_index):
    requests = context_len.shape[0]
    tokens = cache.shape[2]
    block_live = block_owner < requests
    owner_row = jnp.minimum(block_owner, requests - 1)
    last_position = context_len[owner_row] - 1
    block_hit = block_live & (block_index == last_position // tokens)
    slot_hit = block_hit[:, None] & (jnp.arange(tokens, dtype=jnp.int32)[None, :] == (last_position % tokens)[:, None])
    fresh_rows = jnp.stack([keys_new[owner_row], values_new[owner_row]], axis=1)
    return jnp.where(slot_hit[:, None, :, None], fresh_rows[:, :, None, :], cache)

def partials(query, cache, context_len, block_owner, block_index):
    blocks, _, tokens, columns = cache.shape
    head_count = columns // HEAD_DIM
    requests = context_len.shape[0]
    block_live = block_owner < requests
    owner_row = jnp.minimum(block_owner, requests - 1)
    query_rows = query[owner_row].reshape(blocks, head_count, HEAD_DIM)
    key_cache = cache[:, 0].reshape(blocks, tokens, head_count, HEAD_DIM)
    value_cache = cache[:, 1].reshape(blocks, tokens, head_count, HEAD_DIM)
    scores = jnp.einsum('bhd,bthd->bht', query_rows.astype(jnp.float32), key_cache.astype(jnp.float32))
    token_position = block_index[:, None] * tokens + jnp.arange(tokens, dtype=jnp.int32)[None, :]
    visible = block_live[:, None] & (token_position < context_len[owner_row][:, None])
    masked = jnp.where(visible[:, None, :], scores, NEG_FLOOR)
    block_max = lax.optimization_barrier(jnp.max(masked, axis=-1))
    weights = jnp.where(visible[:, None, :], jnp.exp(masked - block_max[..., None]), 0.0).astype(jnp.bfloat16)
    block_sum = lax.optimization_barrier(jnp.sum(weights.astype(jnp.float32), axis=-1))
    block_out = jnp.einsum('bht,bthd->bhd', weights.astype(jnp.float32), value_cache.astype(jnp.float32)).reshape(blocks, columns)
    return (block_max, block_sum, block_out)

def reference(states, norm_gain, w_qkv, w_out, cache, context_len, block_owner, block_index):
    wide_states = states.astype(jnp.float32)
    inverse = lax.rsqrt(lax.optimization_barrier(jnp.mean(wide_states * wide_states, axis=1, keepdims=True)) + EPSILON)
    normed = (wide_states * inverse * norm_gain.astype(jnp.float32)[None, :]).astype(jnp.bfloat16)
    projected = jnp.stack([jnp.dot(normed, w_qkv[index_c], preferred_element_type=jnp.float32) for index_c in range(3)], axis=1)
    positions = context_len - 1
    query, keys_new, values_new = finish(projected, positions)
    updated = append(cache, keys_new, values_new, context_len, block_owner, block_index)
    shape_group = (N_SEQ, BLOCKS_DEV)

    def group_part(group):
        return partials(query, group[0], context_len, group[1], group[2])
    block_max, block_sum, block_out = lax.map(group_part, (updated.reshape(shape_group + updated.shape[1:]), block_owner.reshape(shape_group), block_index.reshape(shape_group)))
    block_max = block_max.reshape(POOL, -1)
    block_sum = block_sum.reshape(POOL, -1)
    block_out = block_out.reshape(POOL, -1)
    requests = context_len.shape[0]
    block_live = block_owner < requests
    owner_row = jnp.minimum(block_owner, requests - 1)
    segment = jnp.where(block_live, block_owner, requests).astype(jnp.int32)
    member = segment[:, None] == jnp.arange(requests, dtype=jnp.int32)[None, :]
    request_max = lax.optimization_barrier(jnp.max(jnp.where(member[:, :, None], block_max[:, None, :], NEG_FLOOR), axis=0))
    factor = jnp.exp(block_max - request_max[owner_row])
    totals = jax.ops.segment_sum(block_sum * factor, segment, requests + 1)[:requests]
    outputs = jax.ops.segment_sum(block_out * jnp.repeat(factor, HEAD_DIM, axis=1), segment, requests + 1)[:requests]
    attended = (outputs / jnp.repeat(totals, HEAD_DIM, axis=1)).astype(jnp.bfloat16)
    hidden = (jnp.dot(attended, w_out, preferred_element_type=jnp.float32) + wide_states).astype(jnp.bfloat16)
    return (hidden, updated)
```

```python
import functools

import jax
import jax.numpy as jnp
import numpy as np
from jax import lax
from jax.experimental import pallas as pl
from jax.experimental.pallas import tpu as pltpu
from jax.sharding import PartitionSpec as P

HEAD_DIM = 96
EPSILON = 1e-05
NEG_FLOOR = -1e30
GROUP = 8
LANES = 128
SIDE = 4
LONG_LIMIT = 31 * 64
LONG_REQS = 4
SLOTS = 24


def place():
    me = lax.axis_index("seq")
    core = me % 2
    y = (me // 2) % SIDE
    z = me // (2 * SIDE)
    first = z * (1 - core) + y * core
    second = y * (1 - core) + z * core

    def device(a, b):
        zz = a * (1 - core) + b * core
        yy = b * (1 - core) + a * core
        return (zz * SIDE + yy) * 2 + core

    primary = [device((first + i) % SIDE, second) for i in range(1, SIDE)]
    secondary = [device(first, (second + i) % SIDE) for i in range(1, SIDE)]
    partner = me + 1 - 2 * core
    return core, first, second, partner, primary, secondary


def send(src, dst, send_sem, recv_sem, axis, to):
    copy = pltpu.make_async_remote_copy(
        src_ref=src,
        dst_ref=dst,
        send_sem=send_sem,
        recv_sem=recv_sem,
        device_id={axis: to},
        device_id_type=pl.DeviceIdType.MESH,
    )
    copy.start()
    return copy


def greet(axis, others):
    barrier = pltpu.get_barrier_semaphore()
    for other in others:
        pl.semaphore_signal(
            barrier, inc=1, device_id={axis: other}, device_id_type=pl.DeviceIdType.MESH
        )


def halves(total):
    high = total.astype(jnp.bfloat16).astype(jnp.float32)
    lane = lax.broadcasted_iota(jnp.int32, total.shape, total.ndim - 1)
    return jnp.where(lane < LANES // 2, high, total - high).astype(jnp.bfloat16)


def whole(pair):
    pair = pair.astype(jnp.float32)
    return pair + pltpu.roll(pair, LANES // 2, pair.ndim - 1)


def rotated(values, cosine, sine, is_front):
    width = values.shape[-1]
    half = HEAD_DIM // 2
    other = jnp.where(
        is_front, pltpu.roll(values, width - half, 1), pltpu.roll(values, half, 1)
    )
    return values * cosine + other * sine


def project_kernel(
    context_ref, owner_ref, states_ref, gain_ref, w_ref, frequency_ref, out_ref,
    own, snd0, rcv0, snd1, rcv1, snd2, rcv2, gathered,
    sem0, sem1s, sem1r, sem2s, sem2r, sem3s, sem3r, sem4s, sem4r, sem5,
):
    core, first, second, partner, primary, secondary = place()
    greet("seq", [partner] + primary + secondary)

    parts, _, columns = w_ref.shape
    width = parts * columns
    rows = snd0.shape[0] * GROUP

    def local(half):
        rows_ref = states_ref[pl.ds(pl.multiple_of(half * rows, rows), rows), :]
        wide = rows_ref.astype(jnp.float32)
        total = jnp.sum(wide * wide, axis=1, keepdims=True)
        scaled = (wide * gain_ref[...].astype(jnp.float32)).astype(jnp.bfloat16)
        return scaled, jnp.broadcast_to(total, (rows, LANES))

    scaled, total = local(1 - core)
    for part in range(parts):
        term = jnp.dot(scaled, w_ref[part], preferred_element_type=jnp.float32)
        snd0[:, :, part * columns : (part + 1) * columns] = term.reshape(
            rows // GROUP, GROUP, columns
        ).astype(jnp.bfloat16)
    snd0[:, :, width:] = halves(total).reshape(rows // GROUP, GROUP, LANES)
    pl.semaphore_wait(pltpu.get_barrier_semaphore(), 7)
    copy0 = send(snd0, rcv0, sem0.at[0], sem0.at[1], "seq", partner)

    scaled, total = local(core)
    for part in range(parts):
        term = jnp.dot(scaled, w_ref[part], preferred_element_type=jnp.float32)
        own[:, :, part * columns : (part + 1) * columns] = term.reshape(
            rows // GROUP, GROUP, columns
        )
    own[:, :, width:] = total.reshape(rows // GROUP, GROUP, LANES)
    copy0.wait()

    copies = []
    for i in range(1, SIDE):
        there = ((first + i) % SIDE) * SIDE
        chunk = pl.ds(there, SIDE)
        snd1[i - 1, :, :, :width] = (
            own[chunk, :, :width] + rcv0[chunk, :, :width].astype(jnp.float32)
        ).astype(jnp.bfloat16)
        snd1[i - 1, :, :, width:] = halves(own[chunk, :, width:] + whole(rcv0[chunk, :, width:]))
        copies.append(
            send(
                snd1.at[i - 1], rcv1.at[i - 1], sem1s.at[i - 1], sem1r.at[i - 1],
                "seq", primary[i - 1],
            )
        )
    here = (core * SIDE + first) * SIDE + second
    row = lax.broadcasted_iota(jnp.int32, (GROUP, columns), 0)
    position = jnp.zeros((GROUP, columns), jnp.int32)
    for i in range(GROUP):
        position = jnp.where(row == i, context_ref[here * GROUP + i] - 1, position)
    angle = position.astype(jnp.float32) * frequency_ref[...]
    cosine = jnp.cos(angle)
    is_front = lax.broadcasted_iota(jnp.int32, (GROUP, columns), 1) % HEAD_DIM < HEAD_DIM // 2
    sine = jnp.where(is_front, -jnp.sin(angle), jnp.sin(angle))
    slot = lax.broadcasted_iota(jnp.int32, (SLOTS, 32 * GROUP), 0)
    wanted = jnp.zeros((SLOTS, 32 * GROUP), jnp.int32)
    for i in range(SLOTS):
        wanted = jnp.where(slot == i, owner_ref[i], wanted)
    pick = jnp.where(
        lax.broadcasted_iota(jnp.int32, (SLOTS, 32 * GROUP), 1) == wanted, 1.0, 0.0
    ).astype(jnp.bfloat16)

    mine = pl.ds(first * SIDE, SIDE)
    total = own[mine, :, width:] + whole(rcv0[mine, :, width:])
    own[mine, :, :width] = own[mine, :, :width] + rcv0[mine, :, :width].astype(jnp.float32)
    for copy in copies:
        copy.wait()
    for i in range(1, SIDE):
        total = total + whole(rcv1[i - 1, :, :, width:])
    own[mine, :, width:] = total

    base = first * SIDE
    copies = []
    for i in range(1, SIDE):
        there = (second + i) % SIDE
        term = own[base + there, :, :width]
        for k in range(SIDE - 1):
            term = term + rcv1[k, there, :, :width].astype(jnp.float32)
        snd2[i - 1, :, :width] = term.astype(jnp.bfloat16)
        snd2[i - 1, :, width:] = halves(own[base + there, :, width:])
        copies.append(
            send(
                snd2.at[i - 1], rcv2.at[i - 1], sem2s.at[i - 1], sem2r.at[i - 1],
                "seq", secondary[i - 1],
            )
        )
    term = own[base + second, :, :width]
    for k in range(SIDE - 1):
        term = term + rcv1[k, second, :, :width].astype(jnp.float32)
    total = own[base + second, :, width:]
    for copy in copies:
        copy.wait()
    for k in range(SIDE - 1):
        term = term + rcv2[k, :, :width].astype(jnp.float32)
        total = total + whole(rcv2[k, :, width:])
    inverse = lax.rsqrt(total / (HEAD_DIM * 32) + EPSILON)[:, :1]
    query = rotated(term[:, :columns] * inverse, cosine, sine, is_front) * HEAD_DIM ** (-0.5)
    key = rotated(term[:, columns : 2 * columns] * inverse, cosine, sine, is_front)
    value = term[:, 2 * columns :] * inverse
    gathered[core, first, second, :, :columns] = query.astype(jnp.bfloat16)
    gathered[core, first, second, :, columns : 2 * columns] = key.astype(jnp.bfloat16)
    gathered[core, first, second, :, 2 * columns :] = value.astype(jnp.bfloat16)

    block = gathered.at[core, first, second]
    copies = [
        send(block, block, sem3s.at[i], sem3r.at[i], "seq", secondary[i]) for i in range(SIDE - 1)
    ]
    for copy in copies:
        copy.wait()
    block = gathered.at[core, first]
    copies = [
        send(block, block, sem4s.at[i], sem4r.at[i], "seq", primary[i]) for i in range(SIDE - 1)
    ]
    for copy in copies:
        copy.wait()
    block = gathered.at[core]
    copy = send(block, block, sem5.at[0], sem5.at[1], "seq", partner)
    copy.wait()
    for part in range(parts):
        piece = gathered[:, :, :, :, part * columns : (part + 1) * columns]
        piece = piece.astype(jnp.float32).reshape(32 * GROUP, columns).astype(jnp.bfloat16)
        out_ref[:, part * columns : (part + 1) * columns] = jnp.dot(
            pick, piece, preferred_element_type=jnp.float32
        ).astype(jnp.bfloat16)


def attend_kernel(
    context_ref, owner_ref, index_ref, rows_ref, cache_ref, updated_ref, out_ref, stats_ref,
    buffer, scores, sem_in, sem_out,
):
    blocks, _, tokens, columns = cache_ref.shape
    heads = columns // HEAD_DIM
    requests = context_ref.shape[0]
    loads = []
    for j in range(blocks):
        load = pltpu.make_async_copy(cache_ref.at[j], buffer.at[j], sem_in.at[j])
        load.start()
        loads.append(load)
    head_mask = (
        lax.broadcasted_iota(jnp.int32, (heads, columns), 1) // HEAD_DIM
        == lax.broadcasted_iota(jnp.int32, (heads, columns), 0)
    )
    group = 16
    row = lax.broadcasted_iota(jnp.int32, (group, columns), 0)
    lane = lax.broadcasted_iota(jnp.int32, (heads, LANES), 1)
    owners = []
    seen = []
    owner_lanes = jnp.full((heads, LANES), requests, jnp.int32)
    stores = []
    for j in range(blocks):
        owner = owner_ref[j]
        live = owner < requests
        last = context_ref[jnp.minimum(owner, requests - 1)] - 1
        start = index_ref[j] * tokens
        visible = jnp.where(live, last + 1 - start, 0)
        hit = live & (index_ref[j] == last // tokens)
        place_in = last % tokens
        owners.append(owner)
        seen.append(visible)
        owner_lanes = jnp.where(lane == j, owner, owner_lanes)
        base = pl.multiple_of((place_in // group) * group, group)
        target = jnp.where(hit, place_in - base, -1)
        loads[j].wait()
        for c in range(2):
            fresh = rows_ref[j : j + 1, (c + 1) * columns : (c + 2) * columns]
            old = buffer[j, c, pl.ds(base, group), :]
            buffer[j, c, pl.ds(base, group), :] = jnp.where(
                row == target, fresh.astype(jnp.float32), old.astype(jnp.float32)
            ).astype(jnp.bfloat16)
        store = pltpu.make_async_copy(buffer.at[j], updated_ref.at[j], sem_out.at[j])
        store.start()
        stores.append(store)
        query = rows_ref[j : j + 1, :columns].astype(jnp.float32)
        spread = jnp.where(head_mask, query, 0.0).astype(jnp.bfloat16)
        scores[j] = lax.dot_general(
            spread, buffer[j, 0], (((1,), (1,)), ((), ())), preferred_element_type=jnp.float32
        )
    token = lax.broadcasted_iota(jnp.int32, (heads, tokens), 1)
    masked = []
    peaks = jnp.full((heads, LANES), NEG_FLOOR, jnp.float32)
    for j in range(blocks):
        value = jnp.where(token < seen[j], scores[j], NEG_FLOOR)
        masked.append(value)
        peak = jnp.max(value, axis=1, keepdims=True)
        peaks = jnp.where(lane == j, peak, peaks)
    group_peaks = jnp.zeros((heads, LANES), jnp.float32)
    sums = jnp.zeros((heads, LANES), jnp.float32)
    weights = []
    for j in range(blocks):
        same = owner_lanes == owners[j]
        peak = jnp.max(jnp.where(same, peaks, NEG_FLOOR), axis=1, keepdims=True)
        weight = jnp.where(token < seen[j], jnp.exp(masked[j] - peak), 0.0).astype(jnp.bfloat16)
        weights.append(weight)
        group_peaks = jnp.where(lane == j, peak, group_peaks)
        sums = jnp.where(
            lane == j, jnp.sum(weight.astype(jnp.float32), axis=1, keepdims=True), sums
        )
    group_sums = jnp.zeros((heads, LANES), jnp.float32)
    leads = jnp.zeros((heads, LANES), jnp.float32)
    for j in range(blocks):
        same = owner_lanes == owners[j]
        total = jnp.sum(jnp.where(same, sums, 0.0), axis=1, keepdims=True)
        group_sums = jnp.where(lane == j, total, group_sums)
        earlier = jnp.max(jnp.where(same & (lane < j), 1.0, 0.0), axis=1, keepdims=True)
        leads = jnp.where(lane == j, 1.0 - earlier, leads)
        inverse = jnp.where(total > 0.0, 1.0 / jnp.where(total > 0.0, total, 1.0), 0.0)
        piece = jnp.dot(weights[j], buffer[j, 1], preferred_element_type=jnp.float32)
        piece = jnp.where(head_mask, piece * inverse, 0.0)
        out_ref[j : j + 1, :] = jnp.sum(piece, axis=0, keepdims=True).astype(jnp.bfloat16)
    quarter = LANES // 4
    stats = jnp.where(
        lane < quarter,
        group_peaks,
        jnp.where(
            lane < 2 * quarter,
            pltpu.roll(group_sums, quarter, 1),
            jnp.where(
                lane < 3 * quarter,
                pltpu.roll(leads, 2 * quarter, 1),
                pltpu.roll(owner_lanes.astype(jnp.float32), 3 * quarter, 1),
            ),
        ),
    )
    stats_ref[...] = stats
    for store in stores:
        store.wait()


def combine_kernel(
    context_ref, rows_ref, stats_ref, w_ref, states_ref, out_ref,
    pool, table, terms, arrived,
    sem1s, sem1r, sem2s, sem2r, sem3, sem4s, sem4r,
):
    core, first, second, partner, primary, secondary = place()
    tp = lax.axis_index("tp")
    sides = [(tp + i) % SIDE for i in range(1, SIDE)]
    greet("seq", [partner] + primary + secondary)
    greet("tp", sides)
    slots, columns = rows_ref.shape
    heads = columns // HEAD_DIM
    requests = context_ref.shape[0] * context_ref.shape[1]
    padded = pool.shape[3]
    quarter = LANES // 4
    own_rows = pool.at[core, first, second, pl.ds(0, slots)]
    own_rows[...] = rows_ref[...]
    table[core, first, second] = stats_ref[...]
    pool[:, :, :, slots:, :] = jnp.zeros(
        (2, SIDE, SIDE, padded - slots, columns), jnp.bfloat16
    )
    context = context_ref[...]
    ids = lax.broadcasted_iota(jnp.int32, context.shape, 0) * context.shape[1] + (
        lax.broadcasted_iota(jnp.int32, context.shape, 1)
    )
    candidates = jnp.where(context > LONG_LIMIT, ids, -1).astype(jnp.float32)
    long_ids = []
    for _ in range(LONG_REQS):
        top = jnp.max(jnp.max(candidates, axis=1, keepdims=True), axis=0, keepdims=True)
        long_ids.append(top)
        candidates = jnp.where(candidates == top, -1.0, candidates)
    pl.semaphore_wait(pltpu.get_barrier_semaphore(), 10)

    copies = []
    for i in range(SIDE - 1):
        source = pool.at[core, first, second, pl.ds(0, slots)]
        copies.append(send(source, source, sem1s.at[0, i], sem1r.at[0, i], "seq", secondary[i]))
        source = table.at[core, first, second]
        copies.append(send(source, source, sem1s.at[1, i], sem1r.at[1, i], "seq", secondary[i]))
    for copy in copies:
        copy.wait()
    copies = []
    for i in range(SIDE - 1):
        source = pool.at[core, first, :, pl.ds(0, slots)]
        copies.append(send(source, source, sem2s.at[0, i], sem2r.at[0, i], "seq", primary[i]))
        source = table.at[core, first]
        copies.append(send(source, source, sem2s.at[1, i], sem2r.at[1, i], "seq", primary[i]))
    for copy in copies:
        copy.wait()
    source = pool.at[core, :, :, pl.ds(0, slots)]
    copies = [send(source, source, sem3.at[0], sem3.at[1], "seq", partner)]
    source = table.at[core]
    copies.append(send(source, source, sem3.at[2], sem3.at[3], "seq", partner))
    for copy in copies:
        copy.wait()

    lane = lax.broadcasted_iota(jnp.int32, (heads, LANES), 1)
    fields = [[] for _ in range(4)]
    devices = 2 * SIDE * SIDE
    for start in range(0, devices, 4):
        tiles = []
        for k in range(4):
            d = start + k
            tiles.append(table[d // (SIDE * SIDE), (d // SIDE) % SIDE, d % SIDE])
        for f in range(4):
            merged = jnp.zeros((heads, LANES), jnp.float32)
            for k in range(4):
                shift = ((k - f) * quarter) % LANES
                tile = tiles[k] if shift == 0 else pltpu.roll(tiles[k], shift, 1)
                merged = jnp.where(lane // quarter == k, tile, merged)
            fields[f].append(merged)
    peaks, sums, leads, owners = [jnp.concatenate(f, axis=1) for f in fields]
    used = lax.broadcasted_iota(jnp.int32, owners.shape, 1) % quarter < slots
    owners = jnp.where(used, owners, float(requests))

    high_rows = []
    low_rows = []
    is_long = jnp.zeros(owners.shape, jnp.bool_)
    for l in range(LONG_REQS):
        match = owners == long_ids[l]
        is_long = is_long | match
        peak = jnp.max(jnp.where(match, peaks, NEG_FLOOR), axis=1, keepdims=True)
        mass = jnp.where(match, sums * jnp.exp(jnp.where(match, peaks, NEG_FLOOR) - peak), 0.0)
        weight = mass / jnp.sum(jnp.where(match, mass * leads, 0.0), axis=1, keepdims=True)
        high = weight.astype(jnp.bfloat16)
        high_rows.append(high.astype(jnp.float32))
        low_rows.append(weight - high.astype(jnp.float32))
    request = lax.broadcasted_iota(jnp.int32, (requests, owners.shape[1]), 0).astype(jnp.float32)
    short_owner = jnp.where(is_long, float(requests), owners)[:1]
    member = jnp.where(request == short_owner, 1.0, 0.0).astype(jnp.bfloat16)
    extra = jnp.concatenate(high_rows + low_rows, axis=0).astype(jnp.bfloat16)
    values = (
        pool[...].astype(jnp.float32).reshape(devices * padded, columns).astype(jnp.bfloat16)
    )
    attended = jnp.dot(member, values, preferred_element_type=jnp.float32)
    weighted = jnp.dot(extra, values, preferred_element_type=jnp.float32)
    head_mask = (
        lax.broadcasted_iota(jnp.int32, (heads, columns), 1) // HEAD_DIM
        == lax.broadcasted_iota(jnp.int32, (heads, columns), 0)
    )
    row = lax.broadcasted_iota(jnp.int32, (requests, 1), 0).astype(jnp.float32)
    half = LONG_REQS * heads
    for l in range(LONG_REQS):
        both = weighted[l * heads : (l + 1) * heads] + weighted[
            half + l * heads : half + (l + 1) * heads
        ]
        line = jnp.sum(jnp.where(head_mask, both, 0.0), axis=0, keepdims=True)
        attended = jnp.where(row == long_ids[l], line, attended)
    product = jnp.dot(
        attended.astype(jnp.bfloat16), w_ref[...], preferred_element_type=jnp.float32
    )
    share = requests // SIDE
    terms[...] = product.reshape(SIDE, share, product.shape[1])
    copies = [
        send(
            terms.at[sides[i]], arrived.at[i], sem4s.at[i], sem4r.at[i], "tp", sides[i]
        )
        for i in range(SIDE - 1)
    ]
    total = terms[tp] + states_ref[
        pl.ds(pl.multiple_of(tp * share, share), share), :
    ].astype(jnp.float32)
    for copy in copies:
        copy.wait()
    for i in range(SIDE - 1):
        total = total + arrived[i]
    out_ref[...] = total.astype(jnp.bfloat16)


def shards(states, norm_gain, w_qkv, w_out, cache, context_len, block_owner, block_index):
    requests = states.shape[0]
    parts, depth, columns = w_qkv.shape
    width = parts * columns
    wide = width + LANES
    blocks = cache.shape[0]
    heads = columns // HEAD_DIM
    half_dim = HEAD_DIM // 2
    base = 10000.0 ** (-np.arange(half_dim, dtype=np.float64) * 2.0 / HEAD_DIM)
    frequency = jnp.asarray(np.tile(base, 2 * heads).astype(np.float32)[None, :])
    vmem = pl.BlockSpec(memory_space=pltpu.VMEM)
    smem = pl.BlockSpec(memory_space=pltpu.SMEM)
    hbm = pl.BlockSpec(memory_space=pl.ANY)
    dma = pltpu.SemaphoreType.DMA
    bf16 = jnp.bfloat16
    n = SIDE - 1
    rows = pl.pallas_call(
        project_kernel,
        name="project",
        out_shape=jax.ShapeDtypeStruct((blocks, width), bf16),
        in_specs=[smem, smem, vmem, vmem, vmem, vmem],
        out_specs=vmem,
        scratch_shapes=[
            pltpu.VMEM((16, GROUP, wide), jnp.float32),
            pltpu.VMEM((16, GROUP, wide), bf16),
            pltpu.VMEM((16, GROUP, wide), bf16),
            pltpu.VMEM((n, SIDE, GROUP, wide), bf16),
            pltpu.VMEM((n, SIDE, GROUP, wide), bf16),
            pltpu.VMEM((n, GROUP, wide), bf16),
            pltpu.VMEM((n, GROUP, wide), bf16),
            pltpu.VMEM((2, SIDE, SIDE, GROUP, width), bf16),
            dma((2,)),
            dma((n,)), dma((n,)), dma((n,)), dma((n,)),
            dma((n,)), dma((n,)), dma((n,)), dma((n,)),
            dma((2,)),
        ],
        compiler_params=pltpu.CompilerParams(collective_id=0, has_side_effects=True),
    )(context_len, block_owner, states, norm_gain[None, :], w_qkv, frequency)

    updated, slot_rows, stats = pl.pallas_call(
        attend_kernel,
        name="attend",
        out_shape=(
            jax.ShapeDtypeStruct(cache.shape, bf16),
            jax.ShapeDtypeStruct((blocks, columns), bf16),
            jax.ShapeDtypeStruct((heads, LANES), jnp.float32),
        ),
        in_specs=[smem, smem, smem, vmem, hbm],
        out_specs=(hbm, vmem, vmem),
        scratch_shapes=[
            pltpu.VMEM(cache.shape, bf16),
            pltpu.VMEM((blocks, heads, cache.shape[2]), jnp.float32),
            dma((blocks,)),
            dma((blocks,)),
        ],
    )(context_len, block_owner, block_index, rows, cache)

    hidden = pl.pallas_call(
        combine_kernel,
        name="combine",
        out_shape=jax.ShapeDtypeStruct((requests // SIDE, states.shape[1]), bf16),
        in_specs=[vmem] * 5,
        out_specs=vmem,
        scratch_shapes=[
            pltpu.VMEM((2, SIDE, SIDE, LANES // 4, columns), bf16),
            pltpu.VMEM((2, SIDE, SIDE, heads, LANES), jnp.float32),
            pltpu.VMEM((SIDE, requests // SIDE, states.shape[1]), jnp.float32),
            pltpu.VMEM((n, requests // SIDE, states.shape[1]), jnp.float32),
            dma((2, n)), dma((2, n)), dma((2, n)), dma((2, n)),
            dma((4,)),
            dma((n,)), dma((n,)),
        ],
        compiler_params=pltpu.CompilerParams(collective_id=1, has_side_effects=True),
    )(context_len.reshape(2, requests // 2), slot_rows, stats, w_out, states)
    return (hidden, updated)


def solution(mesh):
    return jax.shard_map(
        shards,
        mesh=mesh,
        in_specs=(
            P(None, "seq"),
            P("seq"),
            P(None, "seq", "tp"),
            P("tp", "seq"),
            P("seq", None, None, "tp"),
            P(),
            P("seq"),
            P("seq"),
        ),
        out_specs=(P("tp", "seq"), P("seq", None, None, "tp")),
        check_vma=False,
    )
```

```python
import functools

import jax
import jax.numpy as jnp
import numpy as np
from jax import lax
from jax.experimental import pallas as pl
from jax.experimental.pallas import tpu as pltpu
from jax.sharding import PartitionSpec as P

HEAD_DIM = 96
EPSILON = 1e-05
NEG_FLOOR = -1e30
GROUP = 8
LANES = 128
SIDE = 4
LONG_LIMIT = 31 * 64
LONG_REQS = 4
ORDER = (2, 1, 3)
ARRIVAL = (0, 2, 1)
ROW_GROUP = 16


def place():
    me = lax.axis_index("seq")
    core = me % 2
    y = (me // 2) % SIDE
    z = me // (2 * SIDE)
    first = z * (1 - core) + y * core
    second = y * (1 - core) + z * core

    def device(a, b):
        zz = a * (1 - core) + b * core
        yy = b * (1 - core) + a * core
        return (zz * SIDE + yy) * 2 + core

    primary = [device((first + i) % SIDE, second) for i in range(1, SIDE)]
    secondary = [device(first, (second + i) % SIDE) for i in range(1, SIDE)]
    partner = me + 1 - 2 * core
    return core, first, second, partner, primary, secondary


def send(src, dst, send_sem, recv_sem, axis, to):
    copy = pltpu.make_async_remote_copy(
        src_ref=src,
        dst_ref=dst,
        send_sem=send_sem,
        recv_sem=recv_sem,
        device_id={axis: to},
        device_id_type=pl.DeviceIdType.MESH,
    )
    copy.start()
    return copy


def greet(axis, others):
    barrier = pltpu.get_barrier_semaphore()
    for other in others:
        pl.semaphore_signal(
            barrier, inc=1, device_id={axis: other}, device_id_type=pl.DeviceIdType.MESH
        )


def halves(total):
    high = total.astype(jnp.bfloat16).astype(jnp.float32)
    lane = lax.broadcasted_iota(jnp.int32, total.shape, total.ndim - 1)
    return jnp.where(lane < LANES // 2, high, total - high).astype(jnp.bfloat16)


def whole(pair):
    pair = pair.astype(jnp.float32)
    return pair + pltpu.roll(pair, LANES // 2, pair.ndim - 1)


def rotated(values, cosine, sine, is_front):
    width = values.shape[-1]
    half = HEAD_DIM // 2
    other = jnp.where(
        is_front, pltpu.roll(values, width - half, 1), pltpu.roll(values, half, 1)
    )
    return values * cosine + other * sine


class Gather:
    def __init__(self, ref, sems, where, part=None):
        self.ref, self.part = ref, part
        self.core, self.first, self.second, self.partner, self.primary, self.secondary = where
        self.near_s, self.near_r, self.far_s, self.far_r, self.swap_s, self.swap_r = sems
        self.far = {}
        self.swaps = []

    def view(self, *index):
        if self.part is None:
            return self.ref.at[index]
        fill = (slice(None),) * (3 - len(index))
        return self.ref.at[index + fill + (pl.ds(0, self.part),)]

    def forward(self, i, block):
        for k in range(SIDE - 1):
            self.far[i, k] = send(
                block, block, self.far_s.at[i, k], self.far_r.at[i, k], "seq", self.primary[k]
            )

    def start(self):
        block = self.view(self.core, self.first, self.second)
        self.near = [
            send(block, block, self.near_s.at[i], self.near_r.at[i], "seq", self.secondary[i])
            for i in range(SIDE - 1)
        ]
        self.forward(0, block)

    def relay(self):
        for i in ARRIVAL:
            self.near[i].wait_recv()
            self.forward(
                i + 1,
                self.view(self.core, self.first, (self.second + SIDE - 1 - i) % SIDE),
            )
        self.swap(0, self.view(self.core, self.first))

    def swap(self, k, group):
        self.swaps.append(
            send(group, group, self.swap_s.at[k], self.swap_r.at[k], "seq", self.partner)
        )

    def cross(self):
        for k in ARRIVAL:
            for i in range(SIDE):
                self.far[i, k].wait_recv()
            self.swap(k + 1, self.view(self.core, (self.first + SIDE - 1 - k) % SIDE))

    def finish(self):
        for copy in self.swaps:
            copy.wait_recv()

    def drain(self):
        for copy in self.near + list(self.far.values()) + self.swaps:
            copy.wait_send()


def step_kernel(
    context_hbm, owner_hbm, index_hbm, lens_hbm, states_hbm, gain_hbm, w_hbm, w_out_hbm,
    frequency_hbm, cache_hbm,
    hidden_ref, rows_ref,
    context_ref, owner_ref, index_ref, lens_ref, states_ref, gain_ref, w_ref, w_out_ref,
    frequency_ref, cache, scaled, own, snd0, rcv0, snd1, rcv1, snd2, rcv2, query_pool, fresh_pool, query_rows,
    scores, pool, terms, arrived,
    sem_in, sem0s, sem0r, sem1s, sem1r, sem2s, sem2r,
    q0, q1, q2, q3, q4, q5, k0, k1, k2, k3, k4, k5, o0, o1, o2, o3, o4, o5, sem4s, sem4r,
):
    where = place()
    core, first, second, partner, primary, secondary = where
    tp = lax.axis_index("tp")
    sides = [(tp + i) % SIDE for i in range(1, SIDE)]
    greet("seq", [partner] + primary + secondary)
    greet("tp", sides)
    loads = {}
    for i, (name, source, target) in enumerate(
        (
            ("states", states_hbm, states_ref), ("gain", gain_hbm, gain_ref),
            ("w", w_hbm, w_ref), ("context", context_hbm, context_ref),
            ("owner", owner_hbm, owner_ref), ("index", index_hbm, index_ref),
            ("lens", lens_hbm, lens_ref), ("frequency", frequency_hbm, frequency_ref),
            ("w_out", w_out_hbm, w_out_ref), ("cache", cache_hbm, cache),
        )
    ):
        loads[name] = pltpu.make_async_copy(source, target, sem_in.at[i])
        loads[name].start()

    parts, _, columns = w_ref.shape
    width = parts * columns
    blocks, _, tokens, _ = cache.shape
    heads = columns // HEAD_DIM
    requests = context_ref.shape[0]
    half_rows = requests // 2

    loads["states"].wait()
    loads["gain"].wait()
    states = states_ref[...].astype(jnp.float32).T
    scaled[...] = (states * gain_ref[...].astype(jnp.float32)).astype(jnp.bfloat16)
    squares = jnp.sum(states * states, axis=1, keepdims=True)
    squares = jnp.broadcast_to(squares, (requests, LANES))
    squares = [squares[:half_rows], squares[half_rows:]]
    shape = (SIDE, SIDE, GROUP)
    loads["w"].wait()
    rows = scaled[pl.ds(pl.multiple_of((1 - core) * half_rows, half_rows), half_rows), :]
    for part in range(parts):
        term = jnp.dot(rows, w_ref[part], preferred_element_type=jnp.float32)
        snd0[:, :, :, part * columns : (part + 1) * columns] = term.reshape(
            shape + (columns,)
        ).astype(jnp.bfloat16)
    snd0[:, :, :, width:] = halves(jnp.where(core == 0, squares[1], squares[0])).reshape(
        shape + (LANES,)
    )
    pl.semaphore_wait(pltpu.get_barrier_semaphore(), 10)
    copies0 = {}
    for i in ORDER + (0,):
        chunk = (second + i) % SIDE
        copies0[i] = send(
            snd0.at[chunk], rcv0.at[chunk], sem0s.at[i], sem0r.at[i], "seq", partner
        )
    rows = scaled[pl.ds(pl.multiple_of(core * half_rows, half_rows), half_rows), :]
    for part in range(parts):
        term = jnp.dot(rows, w_ref[part], preferred_element_type=jnp.float32)
        own[:, :, :, part * columns : (part + 1) * columns] = term.reshape(shape + (columns,))
    own[:, :, :, width:] = jnp.where(core == 0, squares[0], squares[1]).reshape(shape + (LANES,))

    copies1 = {}
    for i in ORDER:
        copies0[i].wait_recv()
        a = (first + i) % SIDE
        for j in ORDER + (0,):
            b = (second + j) % SIDE
            snd1[i - 1, j, :, :width] = (
                own[a, b, :, :width] + rcv0[a, b, :, :width].astype(jnp.float32)
            ).astype(jnp.bfloat16)
            snd1[i - 1, j, :, width:] = halves(own[a, b, :, width:] + whole(rcv0[a, b, :, width:]))
            copies1[i, j] = send(
                snd1.at[i - 1, j], rcv1.at[i - 1, j], sem1s.at[i - 1, j], sem1r.at[i - 1, j],
                "seq", primary[i - 1],
            )

    for name in ("context", "owner", "index", "lens", "frequency", "w_out"):
        loads[name].wait()
    here = (core * SIDE + first) * SIDE + second
    row = lax.broadcasted_iota(jnp.int32, (GROUP, columns), 0)
    position = jnp.zeros((GROUP, columns), jnp.int32)
    for i in range(GROUP):
        position = jnp.where(row == i, context_ref[here * GROUP + i] - 1, position)
    angle = position.astype(jnp.float32) * frequency_ref[...]
    cosine = jnp.cos(angle)
    is_front = lax.broadcasted_iota(jnp.int32, (GROUP, columns), 1) % HEAD_DIM < HEAD_DIM // 2
    sine = jnp.sin(angle)
    sine = jnp.where(is_front, -sine, sine)
    slot = lax.broadcasted_iota(jnp.int32, (blocks, requests), 0)
    wanted = jnp.zeros((blocks, requests), jnp.int32)
    lane = lax.broadcasted_iota(jnp.int32, (heads, LANES), 1)
    owner_lanes = jnp.full((heads, LANES), requests, jnp.int32)
    owners, seen, targets = [], [], []
    for j in range(blocks):
        owner = owner_ref[j]
        live = owner < requests
        last = context_ref[jnp.minimum(owner, requests - 1)] - 1
        hit = live & (index_ref[j] == last // tokens)
        wanted = jnp.where(slot == j, owner, wanted)
        owner_lanes = jnp.where(lane == j, owner, owner_lanes)
        owners.append(owner)
        seen.append(jnp.where(live, last + 1 - index_ref[j] * tokens, 0))
        targets.append(jnp.where(hit, last % tokens, -1))
    pick = jnp.where(
        lax.broadcasted_iota(jnp.int32, (blocks, requests), 1) == wanted, 1.0, 0.0
    ).astype(jnp.bfloat16)
    head_mask = (
        lax.broadcasted_iota(jnp.int32, (heads, columns), 1) // HEAD_DIM
        == lax.broadcasted_iota(jnp.int32, (heads, columns), 0)
    )
    pool[:, :, :, blocks:, :] = jnp.zeros(
        (2, SIDE, SIDE, pool.shape[3] - blocks, pool.shape[4]), jnp.bfloat16
    )
    lens = lens_ref[...]
    ids = lax.broadcasted_iota(jnp.int32, lens.shape, 0) * lens.shape[1] + (
        lax.broadcasted_iota(jnp.int32, lens.shape, 1)
    )
    candidates = jnp.where(lens > LONG_LIMIT, ids, -1).astype(jnp.float32)
    long_ids = []
    for _ in range(LONG_REQS):
        top = jnp.max(jnp.max(candidates, axis=1, keepdims=True), axis=0, keepdims=True)
        long_ids.append(top)
        candidates = jnp.where(candidates == top, -1.0, candidates)

    copies0[0].wait_recv()
    copies2 = {}
    for j in ORDER + (0,):
        b = (second + j) % SIDE
        term = own[first, b, :, :width] + rcv0[first, b, :, :width].astype(jnp.float32)
        total = own[first, b, :, width:] + whole(rcv0[first, b, :, width:])
        for i in ORDER:
            copies1[i, j].wait_recv()
            term = term + rcv1[i - 1, j, :, :width].astype(jnp.float32)
            total = total + whole(rcv1[i - 1, j, :, width:])
        if j:
            snd2[j - 1, :, :width] = term.astype(jnp.bfloat16)
            snd2[j - 1, :, width:] = halves(total)
            copies2[j] = send(
                snd2.at[j - 1], rcv2.at[j - 1], sem2s.at[j - 1], sem2r.at[j - 1],
                "seq", secondary[j - 1],
            )
    loads["cache"].wait()
    for j in (1, 3, 2):
        copies2[j].wait_recv()
        term = term + rcv2[j - 1, :, :width].astype(jnp.float32)
        total = total + whole(rcv2[j - 1, :, width:])

    inverse = lax.rsqrt(total / (HEAD_DIM * 32) + EPSILON)[:, :1]
    query = rotated(term[:, :columns] * inverse, cosine, sine, is_front) * HEAD_DIM ** (-0.5)
    query_pool[core, first, second] = query.astype(jnp.bfloat16)
    queries = Gather(query_pool, (q0, q1, q2, q3, q4, q5), where)
    queries.start()
    key = rotated(term[:, columns : 2 * columns] * inverse, cosine, sine, is_front)
    fresh_pool[core, first, second, :, :columns] = key.astype(jnp.bfloat16)
    fresh_pool[core, first, second, :, columns:] = (term[:, 2 * columns :] * inverse).astype(
        jnp.bfloat16
    )
    news = Gather(fresh_pool, (k0, k1, k2, k3, k4, k5), where)
    news.start()
    queries.relay()
    news.relay()
    queries.cross()
    queries.finish()

    def picked(piece):
        piece = piece.astype(jnp.float32).reshape(requests, columns).astype(jnp.bfloat16)
        return jnp.dot(pick, piece, preferred_element_type=jnp.float32)

    query_rows[...] = picked(query_pool[...])
    for j in range(blocks):
        if j == blocks // 2:
            news.cross()
        spread = jnp.where(head_mask, query_rows[j : j + 1, :], 0.0).astype(jnp.bfloat16)
        scores[j] = lax.dot_general(
            spread, cache[j, 0], (((1,), (1,)), ((), ())), preferred_element_type=jnp.float32
        )
    news.finish()
    key_rows = picked(fresh_pool[:, :, :, :, :columns])
    value_rows = picked(fresh_pool[:, :, :, :, columns:])
    product = query_rows[...] * key_rows
    high = product.astype(jnp.bfloat16)
    low = (product - high.astype(jnp.float32)).astype(jnp.bfloat16)
    head_rows = jnp.where(head_mask, 1.0, 0.0).astype(jnp.bfloat16)
    new_scores = sum(
        lax.dot_general(
            head_rows, piece, (((1,), (1,)), ((), ())), preferred_element_type=jnp.float32
        )
        for piece in (high, low)
    )

    token = lax.broadcasted_iota(jnp.int32, (heads, tokens), 1)
    masked = []
    peaks = jnp.full((heads, LANES), NEG_FLOOR, jnp.float32)
    for j in range(blocks):
        value = jnp.where(token == targets[j], new_scores[:, j : j + 1], scores[j])
        value = jnp.where(token < seen[j], value, NEG_FLOOR)
        masked.append(value)
        peaks = jnp.where(lane == j, jnp.max(value, axis=1, keepdims=True), peaks)
    group_peaks = jnp.zeros((heads, LANES), jnp.float32)
    sums = jnp.zeros((heads, LANES), jnp.float32)
    weights, new_weights = [], []
    for j in range(blocks):
        same = owner_lanes == owners[j]
        peak = jnp.max(jnp.where(same, peaks, NEG_FLOOR), axis=1, keepdims=True)
        weight = jnp.where(token < seen[j], jnp.exp(masked[j] - peak), 0.0)
        weight = weight.astype(jnp.bfloat16).astype(jnp.float32)
        is_new = token == targets[j]
        weights.append(jnp.where(is_new, 0.0, weight).astype(jnp.bfloat16))
        new_weights.append(jnp.sum(jnp.where(is_new, weight, 0.0), axis=1, keepdims=True))
        group_peaks = jnp.where(lane == j, peak, group_peaks)
        sums = jnp.where(lane == j, jnp.sum(weight, axis=1, keepdims=True), sums)
    group_sums = jnp.zeros((heads, LANES), jnp.float32)
    leads = jnp.zeros((heads, LANES), jnp.float32)
    lines = []
    for j in range(blocks):
        same = owner_lanes == owners[j]
        total = jnp.sum(jnp.where(same, sums, 0.0), axis=1, keepdims=True)
        group_sums = jnp.where(lane == j, total, group_sums)
        earlier = jnp.max(jnp.where(same & (lane < j), 1.0, 0.0), axis=1, keepdims=True)
        leads = jnp.where(lane == j, 1.0 - earlier, leads)
        inverse = jnp.where(total > 0.0, 1.0 / jnp.where(total > 0.0, total, 1.0), 0.0)
        piece = jnp.dot(weights[j], cache[j, 1], preferred_element_type=jnp.float32)
        piece = piece + new_weights[j] * value_rows[j : j + 1]
        piece = jnp.where(head_mask, piece * inverse, 0.0)
        lines.append(jnp.sum(piece, axis=0, keepdims=True))
    for j in range(0, blocks, GROUP):
        pool[core, first, second, j : j + GROUP, :columns] = jnp.concatenate(
            lines[j : j + GROUP], axis=0
        ).astype(jnp.bfloat16)
    quarter = LANES // 4
    stats = group_peaks
    for f, field in enumerate((group_sums, leads, owner_lanes.astype(jnp.float32))):
        stats = jnp.where(lane // quarter == f + 1, pltpu.roll(field, (f + 1) * quarter, 1), stats)
    for j in range(0, blocks, GROUP):
        piece = stats.astype(jnp.bfloat16)
        pool[core, first, second, j : j + GROUP, columns:] = piece
        stats = stats - piece.astype(jnp.float32)
    outputs = Gather(pool, (o0, o1, o2, o3, o4, o5), where, blocks)
    outputs.start()
    outputs.relay()

    rows_ref[:, :columns] = key_rows.astype(jnp.bfloat16)
    rows_ref[:, columns:] = value_rows.astype(jnp.bfloat16)
    outputs.cross()
    outputs.finish()

    devices = 2 * SIDE * SIDE
    fields = [[] for _ in range(4)]
    for start in range(0, devices, 4):
        tiles = []
        for d in range(start, start + 4):
            tile = pool[
                d // (SIDE * SIDE), d // SIDE % SIDE, d % SIDE, :, columns:
            ].astype(jnp.float32)
            tiles.append(tile[:8] + tile[8:16] + tile[16:24])
        for f in range(4):
            merged = jnp.zeros((heads, LANES), jnp.float32)
            for k in range(4):
                shift = (k - f) * quarter % LANES
                tile = tiles[k] if shift == 0 else pltpu.roll(tiles[k], shift, 1)
                merged = jnp.where(lane // quarter == k, tile, merged)
            fields[f].append(merged)
    peaks, sums, leads, slot_owners = [jnp.concatenate(f, axis=1) for f in fields]
    used = lax.broadcasted_iota(jnp.int32, slot_owners.shape, 1) % quarter < blocks
    slot_owners = jnp.where(used, slot_owners, float(requests))
    high_rows, low_rows = [], []
    is_long = jnp.zeros(slot_owners.shape, jnp.bool_)
    for long_id in long_ids:
        match = slot_owners == long_id
        is_long = is_long | match
        peak = jnp.max(jnp.where(match, peaks, NEG_FLOOR), axis=1, keepdims=True)
        mass = jnp.where(match, sums * jnp.exp(jnp.where(match, peaks, NEG_FLOOR) - peak), 0.0)
        weight = mass / jnp.sum(jnp.where(match, mass * leads, 0.0), axis=1, keepdims=True)
        high = weight.astype(jnp.bfloat16).astype(jnp.float32)
        high_rows.append(high)
        low_rows.append(weight - high)
    request = lax.broadcasted_iota(jnp.int32, (requests, devices * quarter), 0)
    short_owner = jnp.where(is_long, float(requests), slot_owners)[:1]
    member = jnp.where(request.astype(jnp.float32) == short_owner, 1.0, 0.0).astype(jnp.bfloat16)
    extra = jnp.concatenate(high_rows + low_rows, axis=0).astype(jnp.bfloat16)
    values = pool[:, :, :, :, :columns].reshape(devices * quarter, columns)
    attended = jnp.dot(member, values, preferred_element_type=jnp.float32)
    weighted = jnp.dot(extra, values, preferred_element_type=jnp.float32)
    row = lax.broadcasted_iota(jnp.int32, (requests, 1), 0).astype(jnp.float32)
    half = LONG_REQS * heads
    for l, long_id in enumerate(long_ids):
        both = weighted[l * heads : (l + 1) * heads] + weighted[
            half + l * heads : half + (l + 1) * heads
        ]
        line = jnp.sum(jnp.where(head_mask, both, 0.0), axis=0, keepdims=True)
        attended = jnp.where(row == long_id, line, attended)
    result = lax.dot_general(
        attended.astype(jnp.bfloat16), w_out_ref[...], (((1,), (1,)), ((), ())),
        preferred_element_type=jnp.float32,
    )
    share = requests // SIDE
    terms[...] = result.reshape(SIDE, share, result.shape[1])
    copies = [
        send(terms.at[sides[i]], arrived.at[i], sem4s.at[i], sem4r.at[i], "tp", sides[i])
        for i in range(SIDE - 1)
    ]
    pairs = [
        states_ref[:, i * LANES : (i + 1) * LANES].astype(jnp.float32).T
        for i in range(requests // LANES)
    ]
    pair = jnp.where(tp // 2 == 0, pairs[0], pairs[1])
    total = terms[tp] + jnp.where(tp % 2 == 0, pair[:share], pair[share:])
    for copy in copies:
        copy.wait_recv()
    for i in range(SIDE - 1):
        total = total + arrived[i]
    hidden_ref[...] = total.astype(jnp.bfloat16)
    for group in (copies0, copies1, copies2):
        for copy in group.values():
            copy.wait_send()
    for gather in (queries, news, outputs):
        gather.drain()
    for copy in copies:
        copy.wait_send()


def store_kernel(
    context_ref, owner_ref, index_ref, hidden_in_ref, rows_ref, cache_ref,
    hidden_ref, updated_ref, changed, sem,
):
    hidden_ref[...] = hidden_in_ref[...]
    blocks, _, tokens, columns = updated_ref.shape
    requests = context_ref.shape[0]
    groups = tokens // ROW_GROUP
    row = lax.broadcasted_iota(jnp.int32, (ROW_GROUP, columns), 0)
    for j in range(blocks):
        owner = owner_ref[j]
        last = context_ref[jnp.minimum(owner, requests - 1)] - 1
        hit = (owner < requests) & (index_ref[j] == last // tokens)
        place_in = last % tokens

        @pl.when(hit)
        def _(j=j, place_in=place_in):
            group = place_in // ROW_GROUP
            base = pl.multiple_of(group * ROW_GROUP, ROW_GROUP)
            for i in range(1, groups):
                at = pl.ds(pl.multiple_of((group + i) % groups * ROW_GROUP, ROW_GROUP), ROW_GROUP)
                pltpu.make_async_copy(
                    cache_ref.at[j, :, at], updated_ref.at[j, :, at], sem.at[j]
                ).start()
            for c in range(2):
                fresh = rows_ref[j : j + 1, c * columns : (c + 1) * columns]
                old = cache_ref[j, c, pl.ds(base, ROW_GROUP), :]
                changed[j, c] = jnp.where(
                    row == place_in - base, fresh.astype(jnp.float32), old.astype(jnp.float32)
                ).astype(jnp.bfloat16)
            pltpu.make_async_copy(
                changed.at[j], updated_ref.at[j, :, pl.ds(base, ROW_GROUP)], sem.at[j]
            ).start()

        @pl.when(jnp.logical_not(hit))
        def _(j=j):
            pltpu.make_async_copy(cache_ref.at[j], updated_ref.at[j], sem.at[j]).start()

    for j in range(blocks):
        pltpu.make_async_copy(cache_ref.at[j], updated_ref.at[j], sem.at[j]).wait()


def shards(states, norm_gain, w_qkv, w_out, cache, context_len, block_owner, block_index):
    requests, depth = states.shape
    parts, _, columns = w_qkv.shape
    width = parts * columns
    wide = width + LANES
    blocks = cache.shape[0]
    heads = columns // HEAD_DIM
    half_dim = HEAD_DIM // 2
    base = 10000.0 ** (-np.arange(half_dim, dtype=np.float64) * 2.0 / HEAD_DIM)
    frequency = jnp.asarray(np.tile(base, 2 * heads).astype(np.float32)[None, :])
    vmem = pl.BlockSpec(memory_space=pltpu.VMEM)
    smem = pl.BlockSpec(memory_space=pltpu.SMEM)
    hbm = pl.BlockSpec(memory_space=pltpu.HBM)
    dma = pltpu.SemaphoreType.DMA
    bf16 = jnp.bfloat16
    f32 = jnp.float32
    n = SIDE - 1
    share = requests // SIDE
    gather_sems = [dma((n,)), dma((n,)), dma((SIDE, n)), dma((SIDE, n)), dma((SIDE,)), dma((SIDE,))]
    hidden, rows = pl.pallas_call(
        step_kernel,
        name="step",
        out_shape=(
            jax.ShapeDtypeStruct((share, depth), bf16),
            jax.ShapeDtypeStruct((blocks, 2 * columns), bf16),
        ),
        in_specs=[hbm] * 10,
        out_specs=(vmem, vmem),
        scratch_shapes=[
            pltpu.SMEM((requests,), jnp.int32),
            pltpu.SMEM((blocks,), jnp.int32),
            pltpu.SMEM((blocks,), jnp.int32),
            pltpu.VMEM((2, requests // 2), jnp.int32),
            pltpu.VMEM((depth, requests), bf16),
            pltpu.VMEM((1, depth), bf16),
            pltpu.VMEM(w_qkv.shape, bf16),
            pltpu.VMEM((depth, columns), bf16),
            pltpu.VMEM((1, columns), f32),
            pltpu.VMEM(cache.shape, bf16),
            pltpu.VMEM((requests, depth), bf16),
            pltpu.VMEM((SIDE, SIDE, GROUP, wide), f32),
            pltpu.VMEM((SIDE, SIDE, GROUP, wide), bf16),
            pltpu.VMEM((SIDE, SIDE, GROUP, wide), bf16),
            pltpu.VMEM((n, SIDE, GROUP, wide), bf16),
            pltpu.VMEM((n, SIDE, GROUP, wide), bf16),
            pltpu.VMEM((n, GROUP, wide), bf16),
            pltpu.VMEM((n, GROUP, wide), bf16),
            pltpu.VMEM((2, SIDE, SIDE, GROUP, columns), bf16),
            pltpu.VMEM((2, SIDE, SIDE, GROUP, 2 * columns), bf16),
            pltpu.VMEM((blocks, columns), f32),
            pltpu.VMEM((blocks, heads, cache.shape[2]), f32),
            pltpu.VMEM((2, SIDE, SIDE, LANES // 4, columns + LANES), bf16),
            pltpu.VMEM((SIDE, share, depth), f32),
            pltpu.VMEM((n, share, depth), f32),
            dma((10,)),
            dma((SIDE,)), dma((SIDE,)),
            dma((n, SIDE)), dma((n, SIDE)),
            dma((n,)), dma((n,)),
        ]
        + gather_sems * 3
        + [dma((n,)), dma((n,))],
        compiler_params=pltpu.CompilerParams(
            collective_id=0, has_side_effects=True, vmem_limit_bytes=32 << 20
        ),
        cost_estimate=pl.CostEstimate(
            flops=10**9, bytes_accessed=cache.size * 2, transcendentals=10**5
        ),
    )(
        *(
            pltpu.with_memory_space_constraint(array, pltpu.HBM)
            for array in (
                context_len, block_owner, block_index, context_len.reshape(2, requests // 2),
                states.T, norm_gain[None, :], w_qkv, w_out.T, frequency, cache,
            )
        )
    )
    return pl.pallas_call(
        store_kernel,
        name="store",
        out_shape=(
            jax.ShapeDtypeStruct(hidden.shape, bf16),
            jax.ShapeDtypeStruct(cache.shape, bf16),
        ),
        in_specs=[smem, smem, smem, vmem, vmem, vmem],
        out_specs=(vmem, hbm),
        scratch_shapes=[pltpu.VMEM((blocks, 2, ROW_GROUP, columns), bf16), dma((blocks,))],
        compiler_params=pltpu.CompilerParams(vmem_limit_bytes=16 << 20),
    )(context_len, block_owner, block_index, hidden, rows, cache)


def solution(mesh):
    return jax.shard_map(
        shards,
        mesh=mesh,
        in_specs=(
            P(None, "seq"),
            P("seq"),
            P(None, "seq", "tp"),
            P("tp", "seq"),
            P("seq", None, None, "tp"),
            P(),
            P("seq"),
            P("seq"),
        ),
        out_specs=(P("tp", "seq"), P("seq", None, None, "tp")),
        check_vma=False,
    )
```

```python
import functools

import jax
import jax.numpy as jnp
import numpy as np
from jax import lax
from jax.experimental import pallas as pl
from jax.experimental.pallas import tpu as pltpu
from jax.sharding import PartitionSpec as P

HEAD_DIM = 96
EPSILON = 1e-05
NEG_FLOOR = -1e30
GROUP = 8
LANES = 128
SIDE = 4
LONG_LIMIT = 31 * 64
LONG_REQS = 4
ORDER = (2, 1, 3)
DEPARTURE = (1, 0, 2)
ARRIVAL = (0, 2, 1)
ROW_GROUP = 16


def place():
    me = lax.axis_index("seq")
    core = me % 2
    y = (me // 2) % SIDE
    z = me // (2 * SIDE)
    first = z * (1 - core) + y * core
    second = y * (1 - core) + z * core

    def device(a, b):
        zz = a * (1 - core) + b * core
        yy = b * (1 - core) + a * core
        return (zz * SIDE + yy) * 2 + core

    peers = {
        (i, j): device((first + i) % SIDE, (second + j) % SIDE)
        for i in range(SIDE)
        for j in range(SIDE)
        if (i, j) != (0, 0)
    }
    primary = [peers[i, 0] for i in range(1, SIDE)]
    secondary = [peers[0, j] for j in range(1, SIDE)]
    partner = me + 1 - 2 * core
    return core, first, second, partner, primary, secondary, peers


def send(src, dst, send_sem, recv_sem, axis, to):
    copy = pltpu.make_async_remote_copy(
        src_ref=src,
        dst_ref=dst,
        send_sem=send_sem,
        recv_sem=recv_sem,
        device_id={axis: to},
        device_id_type=pl.DeviceIdType.MESH,
    )
    copy.start()
    return copy


def greet(axis, others):
    barrier = pltpu.get_barrier_semaphore()
    for other in others:
        pl.semaphore_signal(
            barrier, inc=1, device_id={axis: other}, device_id_type=pl.DeviceIdType.MESH
        )


def halves(total):
    high = total.astype(jnp.bfloat16).astype(jnp.float32)
    lane = lax.broadcasted_iota(jnp.int32, total.shape, total.ndim - 1)
    return jnp.where(lane < LANES // 2, high, total - high).astype(jnp.bfloat16)


def whole(pair):
    pair = pair.astype(jnp.float32)
    return pair + pltpu.roll(pair, LANES // 2, pair.ndim - 1)


def rotated(values, cosine, sine, is_front):
    width = values.shape[-1]
    half = HEAD_DIM // 2
    other = jnp.where(
        is_front, pltpu.roll(values, width - half, 1), pltpu.roll(values, half, 1)
    )
    return values * cosine + other * sine


class Reduce:
    def __init__(self, refs, sems, where, squares):
        self.own, self.snd0, self.rcv0, self.snd1, self.rcv1, self.snd2, self.rcv2 = refs
        self.sems = sems
        self.first, self.second, self.partner, self.primary, self.secondary = where[1:6]
        self.squares = squares
        self.width = self.own.shape[-1] - (LANES if squares else 0)
        self.copies = []

    def put(self, ref, index, body, total):
        ref[index + (slice(None), slice(0, self.width))] = body.astype(jnp.bfloat16)
        if self.squares:
            ref[index + (slice(None), slice(self.width, None))] = halves(total)

    def add(self, term, ref, index):
        body, total = term
        body = body + ref[index + (slice(None), slice(0, self.width))].astype(jnp.float32)
        if self.squares:
            total = total + whole(ref[index + (slice(None), slice(self.width, None))])
        return body, total

    def local(self, a, b):
        total = self.own[a, b, :, self.width :] if self.squares else None
        return self.add((self.own[a, b, :, : self.width], total), self.rcv0, (a, b))

    def send(self, src, dst, stage, index, to):
        copy = send(
            src, dst, self.sems[2 * stage].at[index], self.sems[2 * stage + 1].at[index], "seq", to
        )
        self.copies.append(copy)
        return copy

    def swap(self):
        self.swapped = {}
        for i in ORDER + (0,):
            b = (self.first + i) % SIDE
            self.swapped[i] = self.send(self.snd0.at[:, b], self.rcv0.at[:, b], 0, i, self.partner)

    def begin(self):
        self.across = {}
        for j in ORDER + (0,):
            self.swapped[j].wait_recv()
            b = (self.second + j) % SIDE
            for i in ORDER:
                self.put(self.snd1, (i - 1, j), *self.local((self.first + i) % SIDE, b))
                self.across[i, j] = self.send(
                    self.snd1.at[i - 1, j], self.rcv1.at[i - 1, j], 1, (i - 1, j),
                    self.primary[i - 1],
                )

    def middle(self):
        self.along = {}
        for j in ORDER + (0,):
            term = self.local(self.first, (self.second + j) % SIDE)
            for i in ORDER:
                self.across[i, j].wait_recv()
                term = self.add(term, self.rcv1, (i - 1, j))
            if j:
                self.put(self.snd2, (j - 1,), *term)
                self.along[j] = self.send(
                    self.snd2.at[j - 1], self.rcv2.at[j - 1], 2, j - 1, self.secondary[j - 1]
                )
        self.term = term

    def end(self):
        for j in (1, 3, 2):
            self.along[j].wait_recv()
            self.term = self.add(self.term, self.rcv2, (j - 1,))
        return self.term

    def drain(self):
        for copy in self.copies:
            copy.wait_send()


class Gather:
    def __init__(self, ref, sems, where, part=None):
        self.ref, self.part = ref, part
        self.core, self.first, self.second, self.partner, self.primary, self.secondary, _ = where
        self.near_s, self.near_r, self.far_s, self.far_r, self.swap_s, self.swap_r = sems
        self.far = {}
        self.swaps = []

    def view(self, *index):
        if self.part is None:
            return self.ref.at[index]
        fill = (slice(None),) * (3 - len(index))
        return self.ref.at[index + fill + (pl.ds(0, self.part),)]

    def forward(self, i, block):
        for k in DEPARTURE:
            self.far[i, k] = send(
                block, block, self.far_s.at[i, k], self.far_r.at[i, k], "seq", self.primary[k]
            )

    def start(self):
        block = self.view(self.core, self.first, self.second)
        self.near = {
            i: send(block, block, self.near_s.at[i], self.near_r.at[i], "seq", self.secondary[i])
            for i in DEPARTURE
        }
        self.forward(0, block)

    def relay(self):
        for i in ARRIVAL:
            self.near[i].wait_recv()
            self.forward(
                i + 1,
                self.view(self.core, self.first, (self.second + SIDE - 1 - i) % SIDE),
            )
        self.swap(0, self.view(self.core, self.first))

    def swap(self, k, group):
        self.swaps.append(
            send(group, group, self.swap_s.at[k], self.swap_r.at[k], "seq", self.partner)
        )

    def cross(self):
        for k in ARRIVAL:
            for i in range(SIDE):
                self.far[i, k].wait_recv()
            self.swap(k + 1, self.view(self.core, (self.first + SIDE - 1 - k) % SIDE))

    def finish(self):
        for copy in self.swaps:
            copy.wait_recv()

    def drain(self):
        for copy in list(self.near.values()) + list(self.far.values()) + self.swaps:
            copy.wait_send()


class Direct:
    def __init__(self, ref, sems, where):
        self.ref = ref
        self.core, self.first, _, self.partner, _, _, self.peers = where
        self.send_sem, self.recv_sem, self.swap_s, self.swap_r = sems
        self.second = where[2]
        self.swaps = []

    def start(self):
        block = self.ref.at[self.core, self.first, self.second]
        far = lambda at: min(at[0], SIDE - at[0]) + min(at[1], SIDE - at[1])
        self.copies = {
            at: send(
                block, block, self.send_sem.at[at], self.recv_sem.at[at], "seq", self.peers[at]
            )
            for at in sorted(self.peers, key=far, reverse=True)
        }

    def cross(self, groups):
        for i in groups:
            for j in range(SIDE):
                if (i, j) != (0, 0):
                    self.copies[i, j].wait_recv()
            group = self.ref.at[self.core, (self.first + SIDE - i) % SIDE]
            self.swaps.append(
                send(group, group, self.swap_s.at[i], self.swap_r.at[i], "seq", self.partner)
            )

    def finish(self):
        for copy in self.swaps:
            copy.wait_recv()

    def drain(self):
        for copy in list(self.copies.values()) + self.swaps:
            copy.wait_send()


def thirds(value):
    pieces = []
    for _ in range(3):
        piece = value.astype(jnp.bfloat16).astype(jnp.float32)
        pieces.append(piece)
        value = value - piece
    return jnp.concatenate(pieces, axis=0)


def step_kernel(
    context_hbm, owner_hbm, index_hbm, lens_hbm, states_hbm, gain_hbm, w_hbm, w_out_hbm,
    frequency_hbm, cache_hbm,
    hidden_ref, rows_ref,
    context_ref, owner_ref, index_ref, lens_ref, states_ref, gain_ref, w_ref, w_out_ref,
    frequency_ref, cache, scaled, a0, a1, a2, a3, a4, a5, a6, b0, b1, b2, b3, b4, b5, b6, query_pool, fresh_pool, query_rows,
    scores, pool, exact, terms, arrived,
    sem_in, c0, c1, c2, c3, c4, c5, d0, d1, d2, d3, d4, d5,
    q0, q1, q2, q3, k0, k1, k2, k3, k4, k5, o0, o1, o2, o3, o4, o5, sem4s, sem4r,
):
    where = place()
    core, first, second, partner, primary, secondary, peers = where
    tp = lax.axis_index("tp")
    sides = [(tp + i) % SIDE for i in range(1, SIDE)]
    greet("seq", [partner] + list(peers.values()))
    greet("tp", sides)
    loads = {}
    for i, (name, source, target) in enumerate(
        (
            ("states", states_hbm, states_ref), ("gain", gain_hbm, gain_ref),
            ("w", w_hbm, w_ref), ("context", context_hbm, context_ref),
            ("owner", owner_hbm, owner_ref), ("index", index_hbm, index_ref),
            ("lens", lens_hbm, lens_ref), ("frequency", frequency_hbm, frequency_ref),
            ("w_out", w_out_hbm, w_out_ref), ("cache", cache_hbm, cache),
        )
    ):
        loads[name] = pltpu.make_async_copy(source, target, sem_in.at[i])
        loads[name].start()

    parts, _, columns = w_ref.shape
    blocks, _, tokens, _ = cache.shape
    heads = columns // HEAD_DIM
    requests = context_ref.shape[0]
    half_rows = requests // 2

    loads["states"].wait()
    loads["gain"].wait()
    states = states_ref[...].astype(jnp.float32).T
    scaled[...] = (states * gain_ref[...].astype(jnp.float32)).astype(jnp.bfloat16)
    squares = jnp.sum(states * states, axis=1, keepdims=True)
    squares = jnp.broadcast_to(squares, (requests, LANES))
    squares = [squares[:half_rows], squares[half_rows:]]
    shape = (SIDE, SIDE, GROUP)
    loads["w"].wait()
    ahead = Reduce((a0, a1, a2, a3, a4, a5, a6), (c0, c1, c2, c3, c4, c5), where, True)
    behind = Reduce((b0, b1, b2, b3, b4, b5, b6), (d0, d1, d2, d3, d4, d5), where, False)

    def project(ref, side, part, at):
        rows = scaled[pl.ds(pl.multiple_of(side * half_rows, half_rows), half_rows), :]
        term = jnp.dot(rows, w_ref[part], preferred_element_type=jnp.float32)
        ref[:, :, :, at * columns : (at + 1) * columns] = term.reshape(
            shape + (columns,)
        ).astype(ref.dtype)

    project(ahead.snd0, 1 - core, 0, 0)
    ahead.snd0[:, :, :, columns:] = halves(
        jnp.where(core == 0, squares[1], squares[0])
    ).reshape(shape + (LANES,))
    pl.semaphore_wait(pltpu.get_barrier_semaphore(), 19)
    ahead.swap()
    project(ahead.own, core, 0, 0)
    ahead.own[:, :, :, columns:] = jnp.where(core == 0, squares[0], squares[1]).reshape(
        shape + (LANES,)
    )
    project(behind.snd0, 1 - core, 1, 0)
    project(behind.snd0, 1 - core, 2, 1)
    behind.swap()
    ahead.begin()
    project(behind.own, core, 1, 0)
    project(behind.own, core, 2, 1)
    behind.begin()

    for name in ("context", "owner", "index", "lens", "frequency", "w_out"):
        loads[name].wait()
    here = (core * SIDE + first) * SIDE + second
    row = lax.broadcasted_iota(jnp.int32, (GROUP, columns), 0)
    position = jnp.zeros((GROUP, columns), jnp.int32)
    for i in range(GROUP):
        position = jnp.where(row == i, context_ref[here * GROUP + i] - 1, position)
    angle = position.astype(jnp.float32) * frequency_ref[...]
    cosine = jnp.cos(angle)
    is_front = lax.broadcasted_iota(jnp.int32, (GROUP, columns), 1) % HEAD_DIM < HEAD_DIM // 2
    sine = jnp.sin(angle)
    sine = jnp.where(is_front, -sine, sine)
    ahead.middle()
    slot = lax.broadcasted_iota(jnp.int32, (blocks, requests), 0)
    wanted = jnp.zeros((blocks, requests), jnp.int32)
    lane = lax.broadcasted_iota(jnp.int32, (heads, LANES), 1)
    owner_lanes = jnp.full((heads, LANES), requests, jnp.int32)
    owners, seen, targets = [], [], []
    for j in range(blocks):
        owner = owner_ref[j]
        live = owner < requests
        last = context_ref[jnp.minimum(owner, requests - 1)] - 1
        hit = live & (index_ref[j] == last // tokens)
        wanted = jnp.where(slot == j, owner, wanted)
        owner_lanes = jnp.where(lane == j, owner, owner_lanes)
        owners.append(owner)
        seen.append(jnp.where(live, last + 1 - index_ref[j] * tokens, 0))
        targets.append(jnp.where(hit, last % tokens, -1))
    pick = jnp.where(
        lax.broadcasted_iota(jnp.int32, (blocks, requests), 1) == wanted, 1.0, 0.0
    ).astype(jnp.bfloat16)
    head_mask = (
        lax.broadcasted_iota(jnp.int32, (heads, columns), 1) // HEAD_DIM
        == lax.broadcasted_iota(jnp.int32, (heads, columns), 0)
    )
    pool[:, :, :, blocks:, :] = jnp.zeros(
        (2, SIDE, SIDE, pool.shape[3] - blocks, pool.shape[4]), jnp.bfloat16
    )
    lens = lens_ref[...]
    ids = lax.broadcasted_iota(jnp.int32, lens.shape, 0) * lens.shape[1] + (
        lax.broadcasted_iota(jnp.int32, lens.shape, 1)
    )
    candidates = jnp.where(lens > LONG_LIMIT, ids, -1).astype(jnp.float32)
    long_ids = []
    for _ in range(LONG_REQS):
        top = jnp.max(jnp.max(candidates, axis=1, keepdims=True), axis=0, keepdims=True)
        long_ids.append(top)
        candidates = jnp.where(candidates == top, -1.0, candidates)
    loads["cache"].wait()
    behind.middle()
    term, total = ahead.end()

    inverse = lax.rsqrt(total / (HEAD_DIM * 32) + EPSILON)[:, :1]
    query = rotated(term * inverse, cosine, sine, is_front) * HEAD_DIM ** (-0.5)
    query_pool[core, first, second] = query.astype(jnp.bfloat16)
    queries = Direct(query_pool, (q0, q1, q2, q3), where)
    queries.start()
    term, _ = behind.end()
    key = rotated(term[:, :columns] * inverse, cosine, sine, is_front)
    fresh_pool[core, first, second, :, :columns] = key.astype(jnp.bfloat16)
    fresh_pool[core, first, second, :, columns:] = (term[:, columns:] * inverse).astype(
        jnp.bfloat16
    )
    news = Gather(fresh_pool, (k0, k1, k2, k3, k4, k5), where)
    news.start()
    queries.cross((0,))
    news.relay()
    queries.cross((1, 3, 2))
    queries.finish()

    def picked(piece):
        piece = piece.astype(jnp.float32).reshape(requests, columns).astype(jnp.bfloat16)
        return jnp.dot(pick, piece, preferred_element_type=jnp.float32)

    query_rows[...] = picked(query_pool[...])
    for j in range(blocks):
        spread = jnp.where(head_mask, query_rows[j : j + 1, :], 0.0).astype(jnp.bfloat16)
        scores[j] = lax.dot_general(
            spread, cache[j, 0], (((1,), (1,)), ((), ())), preferred_element_type=jnp.float32
        )

    token = lax.broadcasted_iota(jnp.int32, (heads, tokens), 1)
    masked, visible = [], []
    peaks = jnp.full((heads, LANES), NEG_FLOOR, jnp.float32)
    for j in range(blocks):
        visible.append((token < seen[j]) & (token != targets[j]))
        value = jnp.where(visible[j], scores[j], NEG_FLOOR)
        masked.append(value)
        peaks = jnp.where(lane == j, jnp.max(value, axis=1, keepdims=True), peaks)
    group_peaks = jnp.zeros((heads, LANES), jnp.float32)
    sums = jnp.zeros((heads, LANES), jnp.float32)
    weights = []
    for j in range(blocks):
        same = owner_lanes == owners[j]
        peak = jnp.max(jnp.where(same, peaks, NEG_FLOOR), axis=1, keepdims=True)
        weights.append(
            jnp.where(visible[j], jnp.exp(masked[j] - peak), 0.0).astype(jnp.bfloat16)
        )
        weight = weights[j].astype(jnp.float32)
        group_peaks = jnp.where(lane == j, peak, group_peaks)
        sums = jnp.where(lane == j, jnp.sum(weight, axis=1, keepdims=True), sums)
    group_sums = jnp.zeros((heads, LANES), jnp.float32)
    leads = jnp.zeros((heads, LANES), jnp.float32)
    lines = []
    for j in range(blocks):
        same = owner_lanes == owners[j]
        total = jnp.sum(jnp.where(same, sums, 0.0), axis=1, keepdims=True)
        group_sums = jnp.where(lane == j, total, group_sums)
        earlier = jnp.max(jnp.where(same & (lane < j), 1.0, 0.0), axis=1, keepdims=True)
        leads = jnp.where(lane == j, 1.0 - earlier, leads)
        inverse = jnp.where(total > 0.0, 1.0 / jnp.where(total > 0.0, total, 1.0), 0.0)
        piece = jnp.dot(weights[j], cache[j, 1], preferred_element_type=jnp.float32)
        piece = jnp.where(head_mask, piece * inverse, 0.0)
        lines.append(jnp.sum(piece, axis=0, keepdims=True))
    for j in range(0, blocks, GROUP):
        pool[core, first, second, j : j + GROUP, :columns] = jnp.concatenate(
            lines[j : j + GROUP], axis=0
        ).astype(jnp.bfloat16)
    quarter = LANES // 4
    stats = group_peaks
    for f, field in enumerate((group_sums, leads, owner_lanes.astype(jnp.float32))):
        stats = jnp.where(lane // quarter == f + 1, pltpu.roll(field, (f + 1) * quarter, 1), stats)
    for j in range(0, blocks, GROUP):
        piece = stats.astype(jnp.bfloat16)
        pool[core, first, second, j : j + GROUP, columns:] = piece
        stats = stats - piece.astype(jnp.float32)
    outputs = Gather(pool, (o0, o1, o2, o3, o4, o5), where, blocks)
    outputs.start()
    news.cross()
    outputs.relay()
    news.finish()

    for part in range(2):
        at = slice(part * columns, (part + 1) * columns)
        rows_ref[:, at] = picked(fresh_pool[:, :, :, :, at]).astype(jnp.bfloat16)
    head_rows = jnp.where(head_mask, 1.0, 0.0).astype(jnp.bfloat16)
    product = query_pool[...].astype(jnp.float32) * fresh_pool[:, :, :, :, :columns].astype(
        jnp.float32
    )
    product = product.reshape(requests, columns)
    high = product.astype(jnp.bfloat16)
    low = (product - high.astype(jnp.float32)).astype(jnp.bfloat16)
    new_scores = sum(
        lax.dot_general(
            head_rows, piece, (((1,), (1,)), ((), ())), preferred_element_type=jnp.float32
        )
        for piece in (high, low)
    )
    outputs.cross()

    devices = SIDE * SIDE
    request = lax.broadcasted_iota(jnp.int32, (requests, devices * quarter), 0).astype(jnp.float32)

    def side(c):
        fields = [[] for _ in range(4)]
        for start in range(0, devices, 4):
            tiles = []
            for d in range(start, start + 4):
                tile = pool[c, d // SIDE, d % SIDE, :, columns:].astype(jnp.float32)
                tiles.append(tile[:8] + tile[8:16] + tile[16:24])
            for f in range(4):
                merged = jnp.zeros((heads, LANES), jnp.float32)
                for k in range(4):
                    shift = (k - f) * quarter % LANES
                    tile = tiles[k] if shift == 0 else pltpu.roll(tiles[k], shift, 1)
                    merged = jnp.where(lane // quarter == k, tile, merged)
                fields[f].append(merged)
        fields = [jnp.concatenate(f, axis=1) for f in fields]
        used = lax.broadcasted_iota(jnp.int32, fields[3].shape, 1) % quarter < blocks
        fields[3] = jnp.where(used, fields[3], float(requests))
        is_long = jnp.zeros(fields[3].shape, jnp.bool_)
        for long_id in long_ids:
            is_long = is_long | (fields[3] == long_id)
        short_owner = jnp.where(is_long, float(requests), fields[3])[:1]
        member = jnp.where(request == short_owner, 1.0, 0.0).astype(jnp.bfloat16)
        values = pool[c, :, :, :, :columns].reshape(devices * quarter, columns)
        led = jnp.concatenate(
            [thirds(jnp.where(fields[2] > 0.5, fields[f], 0.0)) for f in range(2)], axis=0
        ).astype(jnp.bfloat16)
        by_request = lax.dot_general(
            led, member, (((1,), (1,)), ((), ())), preferred_element_type=jnp.float32
        )
        rows = jnp.dot(member, values, preferred_element_type=jnp.float32)
        return fields, values, rows, by_request

    near_fields, near_values, attended, by_request = side(core)
    outputs.finish()
    far_fields, far_values, rest, by_request_rest = side(1 - core)
    attended = attended + rest
    by_request = by_request + by_request_rest
    old_peak, old_mass = [
        by_request[i : i + heads]
        + by_request[i + heads : i + 2 * heads]
        + by_request[i + 2 * heads : i + 3 * heads]
        for i in (0, 3 * heads)
    ]
    request_lane = lax.broadcasted_iota(jnp.int32, (heads, requests), 1).astype(jnp.float32)
    peaks, sums, leads, slot_owners = [
        jnp.concatenate(pair, axis=1) for pair in zip(near_fields, far_fields)
    ]
    high_rows, low_rows = [], []
    for long_id in long_ids:
        match = slot_owners == long_id
        peak = jnp.max(jnp.where(match, peaks, NEG_FLOOR), axis=1, keepdims=True)
        mass = jnp.where(match, sums * jnp.exp(jnp.where(match, peaks, NEG_FLOOR) - peak), 0.0)
        whole_mass = jnp.sum(jnp.where(match, mass * leads, 0.0), axis=1, keepdims=True)
        weight = mass / whole_mass
        old_peak = jnp.where(request_lane == long_id, peak, old_peak)
        old_mass = jnp.where(request_lane == long_id, whole_mass, old_mass)
        high = weight.astype(jnp.bfloat16).astype(jnp.float32)
        high_rows.append(high)
        low_rows.append(weight - high)
    extra = jnp.concatenate(high_rows + low_rows, axis=0).astype(jnp.bfloat16)
    split = devices * quarter
    weighted = jnp.dot(
        extra[:, :split], near_values, preferred_element_type=jnp.float32
    ) + jnp.dot(extra[:, split:], far_values, preferred_element_type=jnp.float32)
    row = lax.broadcasted_iota(jnp.int32, (requests, 1), 0).astype(jnp.float32)
    half = LONG_REQS * heads
    for l, long_id in enumerate(long_ids):
        both = weighted[l * heads : (l + 1) * heads] + weighted[
            half + l * heads : half + (l + 1) * heads
        ]
        line = jnp.sum(jnp.where(head_mask, both, 0.0), axis=0, keepdims=True)
        attended = jnp.where(row == long_id, line, attended)
    share = 1.0 / (1.0 + old_mass * jnp.exp(old_peak - new_scores))
    share = jnp.concatenate(
        [share, jnp.zeros((LANES - heads, requests), jnp.float32)], axis=0
    ).T
    head_tall = jnp.concatenate(
        [head_rows.astype(jnp.float32), jnp.zeros((LANES - heads, columns), jnp.float32)], axis=0
    ).astype(jnp.bfloat16)
    high = share.astype(jnp.bfloat16)
    low = (share - high.astype(jnp.float32)).astype(jnp.bfloat16)
    spread = sum(
        jnp.dot(piece, head_tall, preferred_element_type=jnp.float32) for piece in (high, low)
    )
    new_values = fresh_pool[:, :, :, :, columns:].astype(jnp.float32).reshape(requests, columns)
    attended = attended + spread * (new_values - attended)
    result = lax.dot_general(
        attended.astype(jnp.bfloat16), w_out_ref[...], (((1,), (1,)), ((), ())),
        preferred_element_type=jnp.float32,
    )
    share = requests // SIDE
    result = result.reshape(SIDE, share, result.shape[1])
    exact[...] = result
    terms[...] = result.astype(jnp.bfloat16)
    copies = [
        send(terms.at[sides[i]], arrived.at[i], sem4s.at[i], sem4r.at[i], "tp", sides[i])
        for i in range(SIDE - 1)
    ]
    pairs = [
        states_ref[:, i * LANES : (i + 1) * LANES].astype(jnp.float32).T
        for i in range(requests // LANES)
    ]
    pair = jnp.where(tp // 2 == 0, pairs[0], pairs[1])
    total = exact[tp] + jnp.where(tp % 2 == 0, pair[:share], pair[share:])
    for copy in copies:
        copy.wait_recv()
    for i in range(SIDE - 1):
        total = total + arrived[i].astype(jnp.float32)
    hidden_ref[...] = total.astype(jnp.bfloat16)
    for gather in (ahead, behind, queries, news, outputs):
        gather.drain()
    for copy in copies:
        copy.wait_send()


def store_kernel(
    context_ref, owner_ref, index_ref, hidden_in_ref, rows_ref, cache_ref,
    hidden_ref, updated_ref, changed, sem,
):
    hidden_ref[...] = hidden_in_ref[...]
    blocks, _, tokens, columns = updated_ref.shape
    requests = context_ref.shape[0]
    groups = tokens // ROW_GROUP
    row = lax.broadcasted_iota(jnp.int32, (ROW_GROUP, columns), 0)
    for j in range(blocks):
        owner = owner_ref[j]
        last = context_ref[jnp.minimum(owner, requests - 1)] - 1
        hit = (owner < requests) & (index_ref[j] == last // tokens)
        place_in = last % tokens

        @pl.when(hit)
        def _(j=j, place_in=place_in):
            group = place_in // ROW_GROUP
            base = pl.multiple_of(group * ROW_GROUP, ROW_GROUP)
            for i in range(1, groups):
                at = pl.ds(pl.multiple_of((group + i) % groups * ROW_GROUP, ROW_GROUP), ROW_GROUP)
                pltpu.make_async_copy(
                    cache_ref.at[j, :, at], updated_ref.at[j, :, at], sem.at[j]
                ).start()
            for c in range(2):
                fresh = rows_ref[j : j + 1, c * columns : (c + 1) * columns]
                old = cache_ref[j, c, pl.ds(base, ROW_GROUP), :]
                changed[j, c] = jnp.where(
                    row == place_in - base, fresh.astype(jnp.float32), old.astype(jnp.float32)
                ).astype(jnp.bfloat16)
            pltpu.make_async_copy(
                changed.at[j], updated_ref.at[j, :, pl.ds(base, ROW_GROUP)], sem.at[j]
            ).start()

        @pl.when(jnp.logical_not(hit))
        def _(j=j):
            pltpu.make_async_copy(cache_ref.at[j], updated_ref.at[j], sem.at[j]).start()

    for j in range(blocks):
        pltpu.make_async_copy(cache_ref.at[j], updated_ref.at[j], sem.at[j]).wait()


def shards(states, norm_gain, w_qkv, w_out, cache, context_len, block_owner, block_index):
    requests, depth = states.shape
    parts, _, columns = w_qkv.shape
    blocks = cache.shape[0]
    heads = columns // HEAD_DIM
    half_dim = HEAD_DIM // 2
    base = 10000.0 ** (-np.arange(half_dim, dtype=np.float64) * 2.0 / HEAD_DIM)
    frequency = jnp.asarray(np.tile(base, 2 * heads).astype(np.float32)[None, :])
    vmem = pl.BlockSpec(memory_space=pltpu.VMEM)
    smem = pl.BlockSpec(memory_space=pltpu.SMEM)
    hbm = pl.BlockSpec(memory_space=pltpu.HBM)
    dma = pltpu.SemaphoreType.DMA
    bf16 = jnp.bfloat16
    f32 = jnp.float32
    n = SIDE - 1
    share = requests // SIDE

    def reduce_refs(wide):
        return (
            pltpu.VMEM((SIDE, SIDE, GROUP, wide), f32),
            pltpu.VMEM((SIDE, SIDE, GROUP, wide), bf16),
            pltpu.VMEM((SIDE, SIDE, GROUP, wide), bf16),
            pltpu.VMEM((n, SIDE, GROUP, wide), bf16),
            pltpu.VMEM((n, SIDE, GROUP, wide), bf16),
            pltpu.VMEM((n, GROUP, wide), bf16),
            pltpu.VMEM((n, GROUP, wide), bf16),
        )

    gather_sems = [dma((n,)), dma((n,)), dma((SIDE, n)), dma((SIDE, n)), dma((SIDE,)), dma((SIDE,))]
    hidden, rows = pl.pallas_call(
        step_kernel,
        name="step",
        out_shape=(
            jax.ShapeDtypeStruct((share, depth), bf16),
            jax.ShapeDtypeStruct((blocks, 2 * columns), bf16),
        ),
        in_specs=[hbm] * 10,
        out_specs=(vmem, vmem),
        scratch_shapes=[
            pltpu.SMEM((requests,), jnp.int32),
            pltpu.SMEM((blocks,), jnp.int32),
            pltpu.SMEM((blocks,), jnp.int32),
            pltpu.VMEM((2, requests // 2), jnp.int32),
            pltpu.VMEM((depth, requests), bf16),
            pltpu.VMEM((1, depth), bf16),
            pltpu.VMEM(w_qkv.shape, bf16),
            pltpu.VMEM((depth, columns), bf16),
            pltpu.VMEM((1, columns), f32),
            pltpu.VMEM(cache.shape, bf16),
            pltpu.VMEM((requests, depth), bf16),
            *reduce_refs(columns + LANES),
            *reduce_refs(2 * columns),
            pltpu.VMEM((2, SIDE, SIDE, GROUP, columns), bf16),
            pltpu.VMEM((2, SIDE, SIDE, GROUP, 2 * columns), bf16),
            pltpu.VMEM((blocks, columns), f32),
            pltpu.VMEM((blocks, heads, cache.shape[2]), f32),
            pltpu.VMEM((2, SIDE, SIDE, LANES // 4, columns + LANES), bf16),
            pltpu.VMEM((SIDE, share, depth), f32),
            pltpu.VMEM((SIDE, share, depth), bf16),
            pltpu.VMEM((n, share, depth), bf16),
            dma((10,)),
        ]
        + [
            dma((SIDE,)), dma((SIDE,)),
            dma((n, SIDE)), dma((n, SIDE)),
            dma((n,)), dma((n,)),
        ] * 2
        + [dma((SIDE, SIDE)), dma((SIDE, SIDE)), dma((SIDE,)), dma((SIDE,))]
        + gather_sems * 2
        + [dma((n,)), dma((n,))],
        compiler_params=pltpu.CompilerParams(
            collective_id=0, has_side_effects=True, vmem_limit_bytes=32 << 20
        ),
        cost_estimate=pl.CostEstimate(
            flops=10**9, bytes_accessed=cache.size * 2, transcendentals=10**5
        ),
    )(
        *(
            pltpu.with_memory_space_constraint(array, pltpu.HBM)
            for array in (
                context_len, block_owner, block_index, context_len.reshape(2, requests // 2),
                states.T, norm_gain[None, :], w_qkv, w_out.T, frequency, cache,
            )
        )
    )
    return pl.pallas_call(
        store_kernel,
        name="store",
        out_shape=(
            jax.ShapeDtypeStruct(hidden.shape, bf16),
            jax.ShapeDtypeStruct(cache.shape, bf16),
        ),
        in_specs=[smem, smem, smem, vmem, vmem, vmem],
        out_specs=(vmem, hbm),
        scratch_shapes=[pltpu.VMEM((blocks, 2, ROW_GROUP, columns), bf16), dma((blocks,))],
        compiler_params=pltpu.CompilerParams(vmem_limit_bytes=16 << 20),
    )(context_len, block_owner, block_index, hidden, rows, cache)


def solution(mesh):
    return jax.shard_map(
        shards,
        mesh=mesh,
        in_specs=(
            P(None, "seq"),
            P("seq"),
            P(None, "seq", "tp"),
            P("tp", "seq"),
            P("seq", None, None, "tp"),
            P(),
            P("seq"),
            P("seq"),
        ),
        out_specs=(P("tp", "seq"), P("seq", None, None, "tp")),
        check_vma=False,
    )
```

```python
import functools

import jax
import jax.numpy as jnp
import numpy as np
from jax import lax
from jax.experimental import pallas as pl
from jax.experimental.pallas import tpu as pltpu
from jax.sharding import PartitionSpec as P

HEAD_DIM = 96
EPSILON = 1e-05
NEG_FLOOR = -1e30
GROUP = 8
LANES = 128
SIDE = 4
LONG_LIMIT = 31 * 64
LONG_REQS = 4
ORDER = (2, 1, 3)
DEPARTURE = (1, 0, 2)
ARRIVAL = (0, 2, 1)
ROW_GROUP = 16


def place():
    me = lax.axis_index("seq")
    core = me % 2
    y = (me // 2) % SIDE
    z = me // (2 * SIDE)
    first = z * (1 - core) + y * core
    second = y * (1 - core) + z * core

    def device(a, b):
        zz = a * (1 - core) + b * core
        yy = b * (1 - core) + a * core
        return (zz * SIDE + yy) * 2 + core

    peers = {
        (i, j): device((first + i) % SIDE, (second + j) % SIDE)
        for i in range(SIDE)
        for j in range(SIDE)
        if (i, j) != (0, 0)
    }
    primary = [peers[i, 0] for i in range(1, SIDE)]
    secondary = [peers[0, j] for j in range(1, SIDE)]
    partner = me + 1 - 2 * core
    return core, first, second, partner, primary, secondary, peers


def send(src, dst, send_sem, recv_sem, axis, to):
    copy = pltpu.make_async_remote_copy(
        src_ref=src,
        dst_ref=dst,
        send_sem=send_sem,
        recv_sem=recv_sem,
        device_id={axis: to},
        device_id_type=pl.DeviceIdType.MESH,
    )
    copy.start()
    return copy


def greet(axis, others):
    barrier = pltpu.get_barrier_semaphore()
    for other in others:
        pl.semaphore_signal(
            barrier, inc=1, device_id={axis: other}, device_id_type=pl.DeviceIdType.MESH
        )


def halves(total):
    high = total.astype(jnp.bfloat16).astype(jnp.float32)
    lane = lax.broadcasted_iota(jnp.int32, total.shape, total.ndim - 1)
    return jnp.where(lane < LANES // 2, high, total - high).astype(jnp.bfloat16)


def whole(pair):
    pair = pair.astype(jnp.float32)
    return pair + pltpu.roll(pair, LANES // 2, pair.ndim - 1)


def rotated(values, cosine, sine, is_front):
    width = values.shape[-1]
    half = HEAD_DIM // 2
    other = jnp.where(
        is_front, pltpu.roll(values, width - half, 1), pltpu.roll(values, half, 1)
    )
    return values * cosine + other * sine


class Reduce:
    def __init__(self, refs, sems, where, squares):
        self.own, self.snd0, self.rcv0, self.snd1, self.rcv1, self.snd2, self.rcv2 = refs
        self.sems = sems
        self.first, self.second, self.partner, self.primary, self.secondary = where[1:6]
        self.squares = squares
        self.width = self.own.shape[-1] - (LANES if squares else 0)
        self.copies = []

    def put(self, ref, index, body, total):
        ref[index + (slice(None), slice(0, self.width))] = body.astype(jnp.bfloat16)
        if self.squares:
            ref[index + (slice(None), slice(self.width, None))] = halves(total)

    def add(self, term, ref, index):
        body, total = term
        body = body + ref[index + (slice(None), slice(0, self.width))].astype(jnp.float32)
        if self.squares:
            total = total + whole(ref[index + (slice(None), slice(self.width, None))])
        return body, total

    def local(self, a, b):
        total = self.own[a, b, :, self.width :] if self.squares else None
        return self.add((self.own[a, b, :, : self.width], total), self.rcv0, (a, b))

    def send(self, src, dst, stage, index, to):
        copy = send(
            src, dst, self.sems[2 * stage].at[index], self.sems[2 * stage + 1].at[index], "seq", to
        )
        self.copies.append(copy)
        return copy

    def swap(self):
        self.swapped = {}
        for i in ORDER + (0,):
            b = (self.first + i) % SIDE
            self.swapped[i] = self.send(self.snd0.at[:, b], self.rcv0.at[:, b], 0, i, self.partner)

    def begin(self):
        self.across = {}
        for j in ORDER + (0,):
            self.swapped[j].wait_recv()
            b = (self.second + j) % SIDE
            for i in ORDER:
                self.put(self.snd1, (i - 1, j), *self.local((self.first + i) % SIDE, b))
                self.across[i, j] = self.send(
                    self.snd1.at[i - 1, j], self.rcv1.at[i - 1, j], 1, (i - 1, j),
                    self.primary[i - 1],
                )

    def middle(self):
        self.along = {}
        for j in ORDER + (0,):
            term = self.local(self.first, (self.second + j) % SIDE)
            for i in ORDER:
                self.across[i, j].wait_recv()
                term = self.add(term, self.rcv1, (i - 1, j))
            if j:
                self.put(self.snd2, (j - 1,), *term)
                self.along[j] = self.send(
                    self.snd2.at[j - 1], self.rcv2.at[j - 1], 2, j - 1, self.secondary[j - 1]
                )
        self.term = term

    def end(self):
        for j in (1, 3, 2):
            self.along[j].wait_recv()
            self.term = self.add(self.term, self.rcv2, (j - 1,))
        return self.term

    def drain(self):
        for copy in self.copies:
            copy.wait_send()


class Gather:
    def __init__(self, ref, sems, where, part=None):
        self.ref, self.part = ref, part
        self.core, self.first, self.second, self.partner, self.primary, self.secondary, _ = where
        self.near_s, self.near_r, self.far_s, self.far_r, self.swap_s, self.swap_r = sems
        self.far = {}
        self.swaps = []

    def view(self, *index):
        if self.part is None:
            return self.ref.at[index]
        fill = (slice(None),) * (3 - len(index))
        return self.ref.at[index + fill + (pl.ds(0, self.part),)]

    def forward(self, i, block):
        for k in DEPARTURE:
            self.far[i, k] = send(
                block, block, self.far_s.at[i, k], self.far_r.at[i, k], "seq", self.primary[k]
            )

    def start(self):
        block = self.view(self.core, self.first, self.second)
        self.near = {
            i: send(block, block, self.near_s.at[i], self.near_r.at[i], "seq", self.secondary[i])
            for i in DEPARTURE
        }
        self.forward(0, block)

    def relay(self):
        for i in ARRIVAL:
            self.near[i].wait_recv()
            self.forward(
                i + 1,
                self.view(self.core, self.first, (self.second + SIDE - 1 - i) % SIDE),
            )
        self.swap(0, self.view(self.core, self.first))

    def swap(self, k, group):
        self.swaps.append(
            send(group, group, self.swap_s.at[k], self.swap_r.at[k], "seq", self.partner)
        )

    def cross(self):
        for k in ARRIVAL:
            for i in range(SIDE):
                self.far[i, k].wait_recv()
            self.swap(k + 1, self.view(self.core, (self.first + SIDE - 1 - k) % SIDE))

    def finish(self):
        for copy in self.swaps:
            copy.wait_recv()

    def drain(self):
        for copy in list(self.near.values()) + list(self.far.values()) + self.swaps:
            copy.wait_send()


class Direct:
    def __init__(self, ref, sems, where):
        self.ref = ref
        self.core, self.first, _, self.partner, _, _, self.peers = where
        self.send_sem, self.recv_sem, self.swap_s, self.swap_r = sems
        self.second = where[2]
        self.swaps = []

    def start(self):
        block = self.ref.at[self.core, self.first, self.second]
        far = lambda at: min(at[0], SIDE - at[0]) + min(at[1], SIDE - at[1])
        self.copies = {
            at: send(
                block, block, self.send_sem.at[at], self.recv_sem.at[at], "seq", self.peers[at]
            )
            for at in sorted(self.peers, key=far, reverse=True)
        }

    def cross(self, groups):
        for i in groups:
            for j in range(SIDE):
                if (i, j) != (0, 0):
                    self.copies[i, j].wait_recv()
            group = self.ref.at[self.core, (self.first + SIDE - i) % SIDE]
            self.swaps.append(
                send(group, group, self.swap_s.at[i], self.swap_r.at[i], "seq", self.partner)
            )

    def finish(self):
        for copy in self.swaps:
            copy.wait_recv()

    def drain(self):
        for copy in list(self.copies.values()) + self.swaps:
            copy.wait_send()


def thirds(value):
    pieces = []
    for _ in range(3):
        piece = value.astype(jnp.bfloat16).astype(jnp.float32)
        pieces.append(piece)
        value = value - piece
    return jnp.concatenate(pieces, axis=0)


def step_kernel(
    context_hbm, owner_hbm, index_hbm, lens_hbm, states_hbm, gain_hbm, w_hbm, w_out_hbm,
    frequency_hbm, cache_hbm,
    hidden_ref, rows_ref,
    context_ref, owner_ref, index_ref, lens_ref, states_ref, gain_ref, w_ref, w_out_ref,
    frequency_ref, cache, scaled, a0, a1, a2, a3, a4, a5, a6, b0, b1, b2, b3, b4, b5, b6, query_pool, fresh_pool, query_rows,
    scores, pool, exact, terms, arrived,
    sem_in, c0, c1, c2, c3, c4, c5, d0, d1, d2, d3, d4, d5,
    q0, q1, q2, q3, k0, k1, k2, k3, k4, k5, o0, o1, o2, o3, o4, o5, sem4s, sem4r,
):
    where = place()
    core, first, second, partner, primary, secondary, peers = where
    tp = lax.axis_index("tp")
    sides = [(tp + i) % SIDE for i in range(1, SIDE)]
    greet("seq", [partner] + primary + secondary)
    greet("tp", sides)
    loads = {}
    for i, (name, source, target) in enumerate(
        (
            ("states", states_hbm, states_ref), ("gain", gain_hbm, gain_ref),
            ("w", w_hbm, w_ref), ("context", context_hbm, context_ref),
            ("owner", owner_hbm, owner_ref), ("index", index_hbm, index_ref),
            ("lens", lens_hbm, lens_ref), ("frequency", frequency_hbm, frequency_ref),
            ("w_out", w_out_hbm, w_out_ref), ("cache", cache_hbm, cache),
        )
    ):
        loads[name] = pltpu.make_async_copy(source, target, sem_in.at[i])
        loads[name].start()

    parts, _, columns = w_ref.shape
    blocks, _, tokens, _ = cache.shape
    heads = columns // HEAD_DIM
    requests = context_ref.shape[0]
    half_rows = requests // 2

    loads["states"].wait()
    loads["gain"].wait()
    states = states_ref[...].astype(jnp.float32).T
    scaled[...] = (states * gain_ref[...].astype(jnp.float32)).astype(jnp.bfloat16)
    squares = jnp.sum(states * states, axis=1, keepdims=True)
    squares = jnp.broadcast_to(squares, (requests, LANES))
    squares = [squares[:half_rows], squares[half_rows:]]
    shape = (SIDE, SIDE, GROUP)
    loads["w"].wait()
    ahead = Reduce((a0, a1, a2, a3, a4, a5, a6), (c0, c1, c2, c3, c4, c5), where, True)
    behind = Reduce((b0, b1, b2, b3, b4, b5, b6), (d0, d1, d2, d3, d4, d5), where, False)

    def project(ref, side, part, at):
        rows = scaled[pl.ds(pl.multiple_of(side * half_rows, half_rows), half_rows), :]
        term = jnp.dot(rows, w_ref[part], preferred_element_type=jnp.float32)
        ref[:, :, :, at * columns : (at + 1) * columns] = term.reshape(
            shape + (columns,)
        ).astype(ref.dtype)

    project(ahead.snd0, 1 - core, 0, 0)
    ahead.snd0[:, :, :, columns:] = halves(
        jnp.where(core == 0, squares[1], squares[0])
    ).reshape(shape + (LANES,))
    pl.semaphore_wait(pltpu.get_barrier_semaphore(), 10)
    ahead.swap()
    project(ahead.own, core, 0, 0)
    ahead.own[:, :, :, columns:] = jnp.where(core == 0, squares[0], squares[1]).reshape(
        shape + (LANES,)
    )
    project(behind.snd0, 1 - core, 1, 0)
    project(behind.snd0, 1 - core, 2, 1)
    behind.swap()
    ahead.begin()
    project(behind.own, core, 1, 0)
    project(behind.own, core, 2, 1)
    behind.begin()

    for name in ("context", "owner", "index", "lens", "frequency", "w_out"):
        loads[name].wait()
    here = (core * SIDE + first) * SIDE + second
    row = lax.broadcasted_iota(jnp.int32, (GROUP, columns), 0)
    position = jnp.zeros((GROUP, columns), jnp.int32)
    for i in range(GROUP):
        position = jnp.where(row == i, context_ref[here * GROUP + i] - 1, position)
    angle = position.astype(jnp.float32) * frequency_ref[...]
    cosine = jnp.cos(angle)
    is_front = lax.broadcasted_iota(jnp.int32, (GROUP, columns), 1) % HEAD_DIM < HEAD_DIM // 2
    sine = jnp.sin(angle)
    sine = jnp.where(is_front, -sine, sine)
    ahead.middle()
    slot = lax.broadcasted_iota(jnp.int32, (blocks, requests), 0)
    wanted = jnp.zeros((blocks, requests), jnp.int32)
    lane = lax.broadcasted_iota(jnp.int32, (heads, LANES), 1)
    owner_lanes = jnp.full((heads, LANES), requests, jnp.int32)
    owners, seen, targets = [], [], []
    for j in range(blocks):
        owner = owner_ref[j]
        live = owner < requests
        last = context_ref[jnp.minimum(owner, requests - 1)] - 1
        hit = live & (index_ref[j] == last // tokens)
        wanted = jnp.where(slot == j, owner, wanted)
        owner_lanes = jnp.where(lane == j, owner, owner_lanes)
        owners.append(owner)
        seen.append(jnp.where(live, last + 1 - index_ref[j] * tokens, 0))
        targets.append(jnp.where(hit, last % tokens, -1))
    pick = jnp.where(
        lax.broadcasted_iota(jnp.int32, (blocks, requests), 1) == wanted, 1.0, 0.0
    ).astype(jnp.bfloat16)
    head_mask = (
        lax.broadcasted_iota(jnp.int32, (heads, columns), 1) // HEAD_DIM
        == lax.broadcasted_iota(jnp.int32, (heads, columns), 0)
    )
    pool[:, :, :, blocks:, :] = jnp.zeros(
        (2, SIDE, SIDE, pool.shape[3] - blocks, pool.shape[4]), jnp.bfloat16
    )
    lens = lens_ref[...]
    ids = lax.broadcasted_iota(jnp.int32, lens.shape, 0) * lens.shape[1] + (
        lax.broadcasted_iota(jnp.int32, lens.shape, 1)
    )
    candidates = jnp.where(lens > LONG_LIMIT, ids, -1).astype(jnp.float32)
    long_ids = []
    for _ in range(LONG_REQS):
        top = jnp.max(jnp.max(candidates, axis=1, keepdims=True), axis=0, keepdims=True)
        long_ids.append(top)
        candidates = jnp.where(candidates == top, -1.0, candidates)
    loads["cache"].wait()
    term, total = ahead.end()

    inverse = lax.rsqrt(total / (HEAD_DIM * 32) + EPSILON)[:, :1]
    query = rotated(term * inverse, cosine, sine, is_front) * HEAD_DIM ** (-0.5)
    query_pool[core, first, second] = query.astype(jnp.bfloat16)
    queries = Direct(query_pool, (q0, q1, q2, q3), where)
    queries.start()
    behind.middle()
    term, _ = behind.end()
    key = rotated(term[:, :columns] * inverse, cosine, sine, is_front)
    fresh_pool[core, first, second, :, :columns] = key.astype(jnp.bfloat16)
    fresh_pool[core, first, second, :, columns:] = (term[:, columns:] * inverse).astype(
        jnp.bfloat16
    )
    news = Gather(fresh_pool, (k0, k1, k2, k3, k4, k5), where)
    news.start()
    queries.cross((0,))
    news.relay()
    queries.cross((1, 3, 2))
    queries.finish()

    def picked(piece):
        piece = piece.astype(jnp.float32).reshape(requests, columns).astype(jnp.bfloat16)
        return jnp.dot(pick, piece, preferred_element_type=jnp.float32)

    query_rows[...] = picked(query_pool[...])
    for j in range(blocks):
        spread = jnp.where(head_mask, query_rows[j : j + 1, :], 0.0).astype(jnp.bfloat16)
        scores[j] = lax.dot_general(
            spread, cache[j, 0], (((1,), (1,)), ((), ())), preferred_element_type=jnp.float32
        )

    token = lax.broadcasted_iota(jnp.int32, (heads, tokens), 1)
    masked, visible = [], []
    peaks = jnp.full((heads, LANES), NEG_FLOOR, jnp.float32)
    for j in range(blocks):
        visible.append((token < seen[j]) & (token != targets[j]))
        value = jnp.where(visible[j], scores[j], NEG_FLOOR)
        masked.append(value)
        peaks = jnp.where(lane == j, jnp.max(value, axis=1, keepdims=True), peaks)
    group_peaks = jnp.zeros((heads, LANES), jnp.float32)
    sums = jnp.zeros((heads, LANES), jnp.float32)
    weights = []
    for j in range(blocks):
        same = owner_lanes == owners[j]
        peak = jnp.max(jnp.where(same, peaks, NEG_FLOOR), axis=1, keepdims=True)
        weights.append(
            jnp.where(visible[j], jnp.exp(masked[j] - peak), 0.0).astype(jnp.bfloat16)
        )
        weight = weights[j].astype(jnp.float32)
        group_peaks = jnp.where(lane == j, peak, group_peaks)
        sums = jnp.where(lane == j, jnp.sum(weight, axis=1, keepdims=True), sums)
    group_sums = jnp.zeros((heads, LANES), jnp.float32)
    leads = jnp.zeros((heads, LANES), jnp.float32)
    lines = []
    for j in range(blocks):
        same = owner_lanes == owners[j]
        total = jnp.sum(jnp.where(same, sums, 0.0), axis=1, keepdims=True)
        group_sums = jnp.where(lane == j, total, group_sums)
        earlier = jnp.max(jnp.where(same & (lane < j), 1.0, 0.0), axis=1, keepdims=True)
        leads = jnp.where(lane == j, 1.0 - earlier, leads)
        inverse = jnp.where(total > 0.0, 1.0 / jnp.where(total > 0.0, total, 1.0), 0.0)
        piece = jnp.dot(weights[j], cache[j, 1], preferred_element_type=jnp.float32)
        piece = jnp.where(head_mask, piece * inverse, 0.0)
        lines.append(jnp.sum(piece, axis=0, keepdims=True))
    for j in range(0, blocks, GROUP):
        pool[core, first, second, j : j + GROUP, :columns] = jnp.concatenate(
            lines[j : j + GROUP], axis=0
        ).astype(jnp.bfloat16)
    quarter = LANES // 4
    stats = group_peaks
    for f, field in enumerate((group_sums, leads, owner_lanes.astype(jnp.float32))):
        stats = jnp.where(lane // quarter == f + 1, pltpu.roll(field, (f + 1) * quarter, 1), stats)
    for j in range(0, blocks, GROUP):
        piece = stats.astype(jnp.bfloat16)
        pool[core, first, second, j : j + GROUP, columns:] = piece
        stats = stats - piece.astype(jnp.float32)
    outputs = Gather(pool, (o0, o1, o2, o3, o4, o5), where, blocks)
    outputs.start()
    news.cross()
    outputs.relay()
    news.finish()

    for part in range(2):
        at = slice(part * columns, (part + 1) * columns)
        rows_ref[:, at] = picked(fresh_pool[:, :, :, :, at]).astype(jnp.bfloat16)
    head_rows = jnp.where(head_mask, 1.0, 0.0).astype(jnp.bfloat16)
    product = query_pool[...].astype(jnp.float32) * fresh_pool[:, :, :, :, :columns].astype(
        jnp.float32
    )
    product = product.reshape(requests, columns)
    high = product.astype(jnp.bfloat16)
    low = (product - high.astype(jnp.float32)).astype(jnp.bfloat16)
    new_scores = sum(
        lax.dot_general(
            head_rows, piece, (((1,), (1,)), ((), ())), preferred_element_type=jnp.float32
        )
        for piece in (high, low)
    )
    outputs.cross()

    devices = SIDE * SIDE
    request = lax.broadcasted_iota(jnp.int32, (requests, devices * quarter), 0).astype(jnp.float32)

    def side(c):
        fields = [[] for _ in range(4)]
        for start in range(0, devices, 4):
            tiles = []
            for d in range(start, start + 4):
                tile = pool[c, d // SIDE, d % SIDE, :, columns:].astype(jnp.float32)
                tiles.append(tile[:8] + tile[8:16] + tile[16:24])
            for f in range(4):
                merged = jnp.zeros((heads, LANES), jnp.float32)
                for k in range(4):
                    shift = (k - f) * quarter % LANES
                    tile = tiles[k] if shift == 0 else pltpu.roll(tiles[k], shift, 1)
                    merged = jnp.where(lane // quarter == k, tile, merged)
                fields[f].append(merged)
        fields = [jnp.concatenate(f, axis=1) for f in fields]
        used = lax.broadcasted_iota(jnp.int32, fields[3].shape, 1) % quarter < blocks
        fields[3] = jnp.where(used, fields[3], float(requests))
        is_long = jnp.zeros(fields[3].shape, jnp.bool_)
        for long_id in long_ids:
            is_long = is_long | (fields[3] == long_id)
        short_owner = jnp.where(is_long, float(requests), fields[3])[:1]
        member = jnp.where(request == short_owner, 1.0, 0.0).astype(jnp.bfloat16)
        values = pool[c, :, :, :, :columns].reshape(devices * quarter, columns)
        led = jnp.concatenate(
            [thirds(jnp.where(fields[2] > 0.5, fields[f], 0.0)) for f in range(2)], axis=0
        ).astype(jnp.bfloat16)
        by_request = lax.dot_general(
            led, member, (((1,), (1,)), ((), ())), preferred_element_type=jnp.float32
        )
        rows = jnp.dot(member, values, preferred_element_type=jnp.float32)
        return fields, values, rows, by_request

    near_fields, near_values, attended, by_request = side(core)
    outputs.finish()
    far_fields, far_values, rest, by_request_rest = side(1 - core)
    attended = attended + rest
    by_request = by_request + by_request_rest
    old_peak, old_mass = [
        by_request[i : i + heads]
        + by_request[i + heads : i + 2 * heads]
        + by_request[i + 2 * heads : i + 3 * heads]
        for i in (0, 3 * heads)
    ]
    request_lane = lax.broadcasted_iota(jnp.int32, (heads, requests), 1).astype(jnp.float32)
    peaks, sums, leads, slot_owners = [
        jnp.concatenate(pair, axis=1) for pair in zip(near_fields, far_fields)
    ]
    high_rows, low_rows = [], []
    for long_id in long_ids:
        match = slot_owners == long_id
        peak = jnp.max(jnp.where(match, peaks, NEG_FLOOR), axis=1, keepdims=True)
        mass = jnp.where(match, sums * jnp.exp(jnp.where(match, peaks, NEG_FLOOR) - peak), 0.0)
        whole_mass = jnp.sum(jnp.where(match, mass * leads, 0.0), axis=1, keepdims=True)
        weight = mass / whole_mass
        old_peak = jnp.where(request_lane == long_id, peak, old_peak)
        old_mass = jnp.where(request_lane == long_id, whole_mass, old_mass)
        high = weight.astype(jnp.bfloat16).astype(jnp.float32)
        high_rows.append(high)
        low_rows.append(weight - high)
    extra = jnp.concatenate(high_rows + low_rows, axis=0).astype(jnp.bfloat16)
    split = devices * quarter
    weighted = jnp.dot(
        extra[:, :split], near_values, preferred_element_type=jnp.float32
    ) + jnp.dot(extra[:, split:], far_values, preferred_element_type=jnp.float32)
    row = lax.broadcasted_iota(jnp.int32, (requests, 1), 0).astype(jnp.float32)
    half = LONG_REQS * heads
    for l, long_id in enumerate(long_ids):
        both = weighted[l * heads : (l + 1) * heads] + weighted[
            half + l * heads : half + (l + 1) * heads
        ]
        line = jnp.sum(jnp.where(head_mask, both, 0.0), axis=0, keepdims=True)
        attended = jnp.where(row == long_id, line, attended)
    share = 1.0 / (1.0 + old_mass * jnp.exp(old_peak - new_scores))
    share = jnp.concatenate(
        [share, jnp.zeros((LANES - heads, requests), jnp.float32)], axis=0
    ).T
    head_tall = jnp.concatenate(
        [head_rows.astype(jnp.float32), jnp.zeros((LANES - heads, columns), jnp.float32)], axis=0
    ).astype(jnp.bfloat16)
    high = share.astype(jnp.bfloat16)
    low = (share - high.astype(jnp.float32)).astype(jnp.bfloat16)
    spread = sum(
        jnp.dot(piece, head_tall, preferred_element_type=jnp.float32) for piece in (high, low)
    )
    new_values = fresh_pool[:, :, :, :, columns:].astype(jnp.float32).reshape(requests, columns)
    attended = attended + spread * (new_values - attended)
    result = lax.dot_general(
        attended.astype(jnp.bfloat16), w_out_ref[...], (((1,), (1,)), ((), ())),
        preferred_element_type=jnp.float32,
    )
    share = requests // SIDE
    result = result.reshape(SIDE, share, result.shape[1])
    exact[...] = result
    terms[...] = result.astype(jnp.bfloat16)
    copies = [
        send(terms.at[sides[i]], arrived.at[i], sem4s.at[i], sem4r.at[i], "tp", sides[i])
        for i in range(SIDE - 1)
    ]
    pairs = [
        states_ref[:, i * LANES : (i + 1) * LANES].astype(jnp.float32).T
        for i in range(requests // LANES)
    ]
    pair = jnp.where(tp // 2 == 0, pairs[0], pairs[1])
    total = exact[tp] + jnp.where(tp % 2 == 0, pair[:share], pair[share:])
    for copy in copies:
        copy.wait_recv()
    for i in range(SIDE - 1):
        total = total + arrived[i].astype(jnp.float32)
    hidden_ref[...] = total.astype(jnp.bfloat16)
    for gather in (ahead, behind, queries, news, outputs):
        gather.drain()
    for copy in copies:
        copy.wait_send()


def store_kernel(
    context_ref, owner_ref, index_ref, hidden_in_ref, rows_ref, cache_ref,
    hidden_ref, updated_ref, changed, sem,
):
    hidden_ref[...] = hidden_in_ref[...]
    blocks, _, tokens, columns = updated_ref.shape
    requests = context_ref.shape[0]
    groups = tokens // ROW_GROUP
    row = lax.broadcasted_iota(jnp.int32, (ROW_GROUP, columns), 0)
    for j in range(blocks):
        owner = owner_ref[j]
        last = context_ref[jnp.minimum(owner, requests - 1)] - 1
        hit = (owner < requests) & (index_ref[j] == last // tokens)
        place_in = last % tokens

        @pl.when(hit)
        def _(j=j, place_in=place_in):
            group = place_in // ROW_GROUP
            base = pl.multiple_of(group * ROW_GROUP, ROW_GROUP)
            for i in range(1, groups):
                at = pl.ds(pl.multiple_of((group + i) % groups * ROW_GROUP, ROW_GROUP), ROW_GROUP)
                pltpu.make_async_copy(
                    cache_ref.at[j, :, at], updated_ref.at[j, :, at], sem.at[j]
                ).start()
            for c in range(2):
                fresh = rows_ref[j : j + 1, c * columns : (c + 1) * columns]
                old = cache_ref[j, c, pl.ds(base, ROW_GROUP), :]
                changed[j, c] = jnp.where(
                    row == place_in - base, fresh.astype(jnp.float32), old.astype(jnp.float32)
                ).astype(jnp.bfloat16)
            pltpu.make_async_copy(
                changed.at[j], updated_ref.at[j, :, pl.ds(base, ROW_GROUP)], sem.at[j]
            ).start()

        @pl.when(jnp.logical_not(hit))
        def _(j=j):
            pltpu.make_async_copy(cache_ref.at[j], updated_ref.at[j], sem.at[j]).start()

    for j in range(blocks):
        pltpu.make_async_copy(cache_ref.at[j], updated_ref.at[j], sem.at[j]).wait()


def shards(states, norm_gain, w_qkv, w_out, cache, context_len, block_owner, block_index):
    requests, depth = states.shape
    parts, _, columns = w_qkv.shape
    blocks = cache.shape[0]
    heads = columns // HEAD_DIM
    half_dim = HEAD_DIM // 2
    base = 10000.0 ** (-np.arange(half_dim, dtype=np.float64) * 2.0 / HEAD_DIM)
    frequency = jnp.asarray(np.tile(base, 2 * heads).astype(np.float32)[None, :])
    vmem = pl.BlockSpec(memory_space=pltpu.VMEM)
    smem = pl.BlockSpec(memory_space=pltpu.SMEM)
    hbm = pl.BlockSpec(memory_space=pltpu.HBM)
    dma = pltpu.SemaphoreType.DMA
    bf16 = jnp.bfloat16
    f32 = jnp.float32
    n = SIDE - 1
    share = requests // SIDE

    def reduce_refs(wide):
        return (
            pltpu.VMEM((SIDE, SIDE, GROUP, wide), f32),
            pltpu.VMEM((SIDE, SIDE, GROUP, wide), bf16),
            pltpu.VMEM((SIDE, SIDE, GROUP, wide), bf16),
            pltpu.VMEM((n, SIDE, GROUP, wide), bf16),
            pltpu.VMEM((n, SIDE, GROUP, wide), bf16),
            pltpu.VMEM((n, GROUP, wide), bf16),
            pltpu.VMEM((n, GROUP, wide), bf16),
        )

    gather_sems = [dma((n,)), dma((n,)), dma((SIDE, n)), dma((SIDE, n)), dma((SIDE,)), dma((SIDE,))]
    hidden, rows = pl.pallas_call(
        step_kernel,
        name="step",
        out_shape=(
            jax.ShapeDtypeStruct((share, depth), bf16),
            jax.ShapeDtypeStruct((blocks, 2 * columns), bf16),
        ),
        in_specs=[hbm] * 10,
        out_specs=(vmem, vmem),
        scratch_shapes=[
            pltpu.SMEM((requests,), jnp.int32),
            pltpu.SMEM((blocks,), jnp.int32),
            pltpu.SMEM((blocks,), jnp.int32),
            pltpu.VMEM((2, requests // 2), jnp.int32),
            pltpu.VMEM((depth, requests), bf16),
            pltpu.VMEM((1, depth), bf16),
            pltpu.VMEM(w_qkv.shape, bf16),
            pltpu.VMEM((depth, columns), bf16),
            pltpu.VMEM((1, columns), f32),
            pltpu.VMEM(cache.shape, bf16),
            pltpu.VMEM((requests, depth), bf16),
            *reduce_refs(columns + LANES),
            *reduce_refs(2 * columns),
            pltpu.VMEM((2, SIDE, SIDE, GROUP, columns), bf16),
            pltpu.VMEM((2, SIDE, SIDE, GROUP, 2 * columns), bf16),
            pltpu.VMEM((blocks, columns), f32),
            pltpu.VMEM((blocks, heads, cache.shape[2]), f32),
            pltpu.VMEM((2, SIDE, SIDE, LANES // 4, columns + LANES), bf16),
            pltpu.VMEM((SIDE, share, depth), f32),
            pltpu.VMEM((SIDE, share, depth), bf16),
            pltpu.VMEM((n, share, depth), bf16),
            dma((10,)),
        ]
        + [
            dma((SIDE,)), dma((SIDE,)),
            dma((n, SIDE)), dma((n, SIDE)),
            dma((n,)), dma((n,)),
        ] * 2
        + [dma((SIDE, SIDE)), dma((SIDE, SIDE)), dma((SIDE,)), dma((SIDE,))]
        + gather_sems * 2
        + [dma((n,)), dma((n,))],
        compiler_params=pltpu.CompilerParams(
            collective_id=0, has_side_effects=True, vmem_limit_bytes=32 << 20
        ),
        cost_estimate=pl.CostEstimate(
            flops=10**9, bytes_accessed=cache.size * 2, transcendentals=10**5
        ),
    )(
        *(
            pltpu.with_memory_space_constraint(array, pltpu.HBM)
            for array in (
                context_len, block_owner, block_index, context_len.reshape(2, requests // 2),
                states.T, norm_gain[None, :], w_qkv, w_out.T, frequency, cache,
            )
        )
    )
    return pl.pallas_call(
        store_kernel,
        name="store",
        out_shape=(
            jax.ShapeDtypeStruct(hidden.shape, bf16),
            jax.ShapeDtypeStruct(cache.shape, bf16),
        ),
        in_specs=[smem, smem, smem, vmem, vmem, vmem],
        out_specs=(vmem, hbm),
        scratch_shapes=[pltpu.VMEM((blocks, 2, ROW_GROUP, columns), bf16), dma((blocks,))],
        compiler_params=pltpu.CompilerParams(vmem_limit_bytes=16 << 20),
    )(context_len, block_owner, block_index, hidden, rows, cache)


def solution(mesh):
    return jax.shard_map(
        shards,
        mesh=mesh,
        in_specs=(
            P(None, "seq"),
            P("seq"),
            P(None, "seq", "tp"),
            P("tp", "seq"),
            P("seq", None, None, "tp"),
            P(),
            P("seq"),
            P("seq"),
        ),
        out_specs=(P("tp", "seq"), P("seq", None, None, "tp")),
        check_vma=False,
    )
```

```python
import functools

import jax
import jax.numpy as jnp
import numpy as np
from jax import lax
from jax.experimental import pallas as pl
from jax.experimental.pallas import tpu as pltpu
from jax.sharding import PartitionSpec as P

HEAD_DIM = 96
EPSILON = 1e-05
NEG_FLOOR = -1e30
GROUP = 8
LANES = 128
SIDE = 4
LONG_LIMIT = 31 * 64
LONG_REQS = 4
ORDER = (2, 1, 3)
DEPARTURE = (1, 0, 2)
ARRIVAL = (0, 2, 1)
ROW_GROUP = 16


def place():
    me = lax.axis_index("seq")
    core = me % 2
    y = (me // 2) % SIDE
    z = me // (2 * SIDE)
    first = z * (1 - core) + y * core
    second = y * (1 - core) + z * core

    def device(a, b):
        zz = a * (1 - core) + b * core
        yy = b * (1 - core) + a * core
        return (zz * SIDE + yy) * 2 + core

    peers = {
        (i, j): device((first + i) % SIDE, (second + j) % SIDE)
        for i in range(SIDE)
        for j in range(SIDE)
        if (i, j) != (0, 0)
    }
    primary = [peers[i, 0] for i in range(1, SIDE)]
    secondary = [peers[0, j] for j in range(1, SIDE)]
    partner = me + 1 - 2 * core
    return core, first, second, partner, primary, secondary, peers


def send(src, dst, send_sem, recv_sem, axis, to):
    copy = pltpu.make_async_remote_copy(
        src_ref=src,
        dst_ref=dst,
        send_sem=send_sem,
        recv_sem=recv_sem,
        device_id={axis: to},
        device_id_type=pl.DeviceIdType.MESH,
    )
    copy.start()
    return copy


def greet(axis, others):
    barrier = pltpu.get_barrier_semaphore()
    for other in others:
        pl.semaphore_signal(
            barrier, inc=1, device_id={axis: other}, device_id_type=pl.DeviceIdType.MESH
        )


def halves(total):
    high = total.astype(jnp.bfloat16).astype(jnp.float32)
    lane = lax.broadcasted_iota(jnp.int32, total.shape, total.ndim - 1)
    return jnp.where(lane < LANES // 2, high, total - high).astype(jnp.bfloat16)


def whole(pair):
    pair = pair.astype(jnp.float32)
    return pair + pltpu.roll(pair, LANES // 2, pair.ndim - 1)


def rotated(values, cosine, sine, is_front):
    width = values.shape[-1]
    half = HEAD_DIM // 2
    other = jnp.where(
        is_front, pltpu.roll(values, width - half, 1), pltpu.roll(values, half, 1)
    )
    return values * cosine + other * sine


class Gather:
    def __init__(self, ref, sems, where, part=None):
        self.ref, self.part = ref, part
        self.core, self.first, self.second, self.partner, self.primary, self.secondary, _ = where
        self.near_s, self.near_r, self.far_s, self.far_r, self.swap_s, self.swap_r = sems
        self.far = {}
        self.swaps = []

    def view(self, *index):
        if self.part is None:
            return self.ref.at[index]
        fill = (slice(None),) * (3 - len(index))
        return self.ref.at[index + fill + (pl.ds(0, self.part),)]

    def forward(self, i, block):
        for k in DEPARTURE:
            self.far[i, k] = send(
                block, block, self.far_s.at[i, k], self.far_r.at[i, k], "seq", self.primary[k]
            )

    def start(self):
        block = self.view(self.core, self.first, self.second)
        self.near = {
            i: send(block, block, self.near_s.at[i], self.near_r.at[i], "seq", self.secondary[i])
            for i in DEPARTURE
        }
        self.forward(0, block)

    def relay(self):
        for i in ARRIVAL:
            self.near[i].wait_recv()
            self.forward(
                i + 1,
                self.view(self.core, self.first, (self.second + SIDE - 1 - i) % SIDE),
            )
        self.swap(0, self.view(self.core, self.first))

    def swap(self, k, group):
        self.swaps.append(
            send(group, group, self.swap_s.at[k], self.swap_r.at[k], "seq", self.partner)
        )

    def cross(self):
        for k in ARRIVAL:
            for i in range(SIDE):
                self.far[i, k].wait_recv()
            self.swap(k + 1, self.view(self.core, (self.first + SIDE - 1 - k) % SIDE))

    def finish(self):
        for copy in self.swaps:
            copy.wait_recv()

    def drain(self):
        for copy in list(self.near.values()) + list(self.far.values()) + self.swaps:
            copy.wait_send()


class Direct:
    def __init__(self, ref, sems, where):
        self.ref = ref
        self.core, self.first, _, self.partner, _, _, self.peers = where
        self.send_sem, self.recv_sem, self.swap_s, self.swap_r = sems
        self.second = where[2]
        self.swaps = []

    def start(self):
        block = self.ref.at[self.core, self.first, self.second]
        far = lambda at: min(at[0], SIDE - at[0]) + min(at[1], SIDE - at[1])
        self.copies = {
            at: send(
                block, block, self.send_sem.at[at], self.recv_sem.at[at], "seq", self.peers[at]
            )
            for at in sorted(self.peers, key=far, reverse=True)
        }

    def cross(self, groups):
        for i in groups:
            for j in range(SIDE):
                if (i, j) != (0, 0):
                    self.copies[i, j].wait_recv()
            group = self.ref.at[self.core, (self.first + SIDE - i) % SIDE]
            self.swaps.append(
                send(group, group, self.swap_s.at[i], self.swap_r.at[i], "seq", self.partner)
            )

    def finish(self):
        for copy in self.swaps:
            copy.wait_recv()

    def drain(self):
        for copy in list(self.copies.values()) + self.swaps:
            copy.wait_send()


def thirds(value):
    pieces = []
    for _ in range(3):
        piece = value.astype(jnp.bfloat16).astype(jnp.float32)
        pieces.append(piece)
        value = value - piece
    return jnp.concatenate(pieces, axis=0)


def step_kernel(
    context_hbm, owner_hbm, index_hbm, lens_hbm, states_hbm, gain_hbm, w_hbm, w_out_hbm,
    frequency_hbm, cache_hbm,
    hidden_ref, rows_ref,
    context_ref, owner_ref, index_ref, lens_ref, states_ref, gain_ref, w_ref, w_out_ref,
    frequency_ref, cache, scaled, own, snd0, rcv0, snd1, rcv1, snd2, rcv2, query_pool, fresh_pool, query_rows,
    scores, table, shares, old, pool, exact, terms, arrived,
    sem_in, sem0s, sem0r, sem1s, sem1r, sem2s, sem2r,
    q0, q1, q2, q3, t0, t1, t2, t3, k0, k1, k2, k3, k4, k5, o0, o1, o2, o3, o4, o5, sem4s, sem4r,
):
    where = place()
    core, first, second, partner, primary, secondary, peers = where
    tp = lax.axis_index("tp")
    sides = [(tp + i) % SIDE for i in range(1, SIDE)]
    greet("seq", [partner] + primary + secondary)
    greet("tp", sides)
    loads = {}
    for i, (name, source, target) in enumerate(
        (
            ("states", states_hbm, states_ref), ("gain", gain_hbm, gain_ref),
            ("w", w_hbm, w_ref), ("context", context_hbm, context_ref),
            ("owner", owner_hbm, owner_ref), ("index", index_hbm, index_ref),
            ("lens", lens_hbm, lens_ref), ("frequency", frequency_hbm, frequency_ref),
            ("w_out", w_out_hbm, w_out_ref), ("cache", cache_hbm, cache),
        )
    ):
        loads[name] = pltpu.make_async_copy(source, target, sem_in.at[i])
        loads[name].start()

    parts, _, columns = w_ref.shape
    width = parts * columns
    blocks, _, tokens, _ = cache.shape
    heads = columns // HEAD_DIM
    requests = context_ref.shape[0]
    half_rows = requests // 2

    loads["states"].wait()
    loads["gain"].wait()
    states = states_ref[...].astype(jnp.float32).T
    scaled[...] = (states * gain_ref[...].astype(jnp.float32)).astype(jnp.bfloat16)
    squares = jnp.sum(states * states, axis=1, keepdims=True)
    squares = jnp.broadcast_to(squares, (requests, LANES))
    squares = [squares[:half_rows], squares[half_rows:]]
    shape = (SIDE, SIDE, GROUP)
    loads["w"].wait()
    rows = scaled[pl.ds(pl.multiple_of((1 - core) * half_rows, half_rows), half_rows), :]
    for part in range(parts):
        term = jnp.dot(rows, w_ref[part], preferred_element_type=jnp.float32)
        snd0[:, :, :, part * columns : (part + 1) * columns] = term.reshape(
            shape + (columns,)
        ).astype(jnp.bfloat16)
    snd0[:, :, :, width:] = halves(jnp.where(core == 0, squares[1], squares[0])).reshape(
        shape + (LANES,)
    )
    pl.semaphore_wait(pltpu.get_barrier_semaphore(), 10)
    copies0 = {}
    for i in ORDER + (0,):
        b = (first + i) % SIDE
        copies0[i] = send(
            snd0.at[:, b], rcv0.at[:, b], sem0s.at[i], sem0r.at[i], "seq", partner
        )
    rows = scaled[pl.ds(pl.multiple_of(core * half_rows, half_rows), half_rows), :]
    for part in range(parts):
        term = jnp.dot(rows, w_ref[part], preferred_element_type=jnp.float32)
        own[:, :, :, part * columns : (part + 1) * columns] = term.reshape(shape + (columns,))
    own[:, :, :, width:] = jnp.where(core == 0, squares[0], squares[1]).reshape(shape + (LANES,))

    copies1 = {}
    for j in ORDER + (0,):
        copies0[j].wait_recv()
        b = (second + j) % SIDE
        for i in ORDER:
            a = (first + i) % SIDE
            snd1[i - 1, j, :, :width] = (
                own[a, b, :, :width] + rcv0[a, b, :, :width].astype(jnp.float32)
            ).astype(jnp.bfloat16)
            snd1[i - 1, j, :, width:] = halves(own[a, b, :, width:] + whole(rcv0[a, b, :, width:]))
            copies1[i, j] = send(
                snd1.at[i - 1, j], rcv1.at[i - 1, j], sem1s.at[i - 1, j], sem1r.at[i - 1, j],
                "seq", primary[i - 1],
            )

    for name in ("context", "owner", "index", "lens", "frequency", "w_out"):
        loads[name].wait()
    here = (core * SIDE + first) * SIDE + second
    row = lax.broadcasted_iota(jnp.int32, (GROUP, columns), 0)
    position = jnp.zeros((GROUP, columns), jnp.int32)
    for i in range(GROUP):
        position = jnp.where(row == i, context_ref[here * GROUP + i] - 1, position)
    angle = position.astype(jnp.float32) * frequency_ref[...]
    cosine = jnp.cos(angle)
    is_front = lax.broadcasted_iota(jnp.int32, (GROUP, columns), 1) % HEAD_DIM < HEAD_DIM // 2
    sine = jnp.sin(angle)
    sine = jnp.where(is_front, -sine, sine)

    copies2 = {}
    for j in ORDER + (0,):
        b = (second + j) % SIDE
        term = own[first, b, :, :width] + rcv0[first, b, :, :width].astype(jnp.float32)
        total = own[first, b, :, width:] + whole(rcv0[first, b, :, width:])
        for i in ORDER:
            copies1[i, j].wait_recv()
            term = term + rcv1[i - 1, j, :, :width].astype(jnp.float32)
            total = total + whole(rcv1[i - 1, j, :, width:])
        if j:
            snd2[j - 1, :, :width] = term.astype(jnp.bfloat16)
            snd2[j - 1, :, width:] = halves(total)
            copies2[j] = send(
                snd2.at[j - 1], rcv2.at[j - 1], sem2s.at[j - 1], sem2r.at[j - 1],
                "seq", secondary[j - 1],
            )
    slot = lax.broadcasted_iota(jnp.int32, (blocks, requests), 0)
    wanted = jnp.zeros((blocks, requests), jnp.int32)
    lane = lax.broadcasted_iota(jnp.int32, (heads, LANES), 1)
    owner_lanes = jnp.full((heads, LANES), requests, jnp.int32)
    owners, seen, targets = [], [], []
    for j in range(blocks):
        owner = owner_ref[j]
        live = owner < requests
        last = context_ref[jnp.minimum(owner, requests - 1)] - 1
        hit = live & (index_ref[j] == last // tokens)
        wanted = jnp.where(slot == j, owner, wanted)
        owner_lanes = jnp.where(lane == j, owner, owner_lanes)
        owners.append(owner)
        seen.append(jnp.where(live, last + 1 - index_ref[j] * tokens, 0))
        targets.append(jnp.where(hit, last % tokens, -1))
    pick = jnp.where(
        lax.broadcasted_iota(jnp.int32, (blocks, requests), 1) == wanted, 1.0, 0.0
    ).astype(jnp.bfloat16)
    head_mask = (
        lax.broadcasted_iota(jnp.int32, (heads, columns), 1) // HEAD_DIM
        == lax.broadcasted_iota(jnp.int32, (heads, columns), 0)
    )
    pool[:, :, :, blocks:, :] = jnp.zeros(
        (2, SIDE, SIDE, pool.shape[3] - blocks, pool.shape[4]), jnp.bfloat16
    )
    lens = lens_ref[...]
    ids = lax.broadcasted_iota(jnp.int32, lens.shape, 0) * lens.shape[1] + (
        lax.broadcasted_iota(jnp.int32, lens.shape, 1)
    )
    candidates = jnp.where(lens > LONG_LIMIT, ids, -1).astype(jnp.float32)
    long_ids = []
    for _ in range(LONG_REQS):
        top = jnp.max(jnp.max(candidates, axis=1, keepdims=True), axis=0, keepdims=True)
        long_ids.append(top)
        candidates = jnp.where(candidates == top, -1.0, candidates)
    loads["cache"].wait()
    for j in (1, 3, 2):
        copies2[j].wait_recv()
        term = term + rcv2[j - 1, :, :width].astype(jnp.float32)
        total = total + whole(rcv2[j - 1, :, width:])

    inverse = lax.rsqrt(total / (HEAD_DIM * 32) + EPSILON)[:, :1]
    query = rotated(term[:, :columns] * inverse, cosine, sine, is_front) * HEAD_DIM ** (-0.5)
    query_pool[core, first, second] = query.astype(jnp.bfloat16)
    queries = Direct(query_pool, (q0, q1, q2, q3), where)
    queries.start()
    key = rotated(term[:, columns : 2 * columns] * inverse, cosine, sine, is_front)
    fresh_pool[core, first, second, :, :columns] = key.astype(jnp.bfloat16)
    fresh_pool[core, first, second, :, columns:] = (term[:, 2 * columns :] * inverse).astype(
        jnp.bfloat16
    )
    news = Gather(fresh_pool, (k0, k1, k2, k3, k4, k5), where)
    news.start()
    queries.cross((0,))
    news.relay()
    queries.cross((1, 3, 2))
    queries.finish()

    def picked(piece):
        piece = piece.astype(jnp.float32).reshape(requests, columns).astype(jnp.bfloat16)
        return jnp.dot(pick, piece, preferred_element_type=jnp.float32)

    query_rows[...] = picked(query_pool[...])
    for j in range(blocks):
        spread = jnp.where(head_mask, query_rows[j : j + 1, :], 0.0).astype(jnp.bfloat16)
        scores[j] = lax.dot_general(
            spread, cache[j, 0], (((1,), (1,)), ((), ())), preferred_element_type=jnp.float32
        )

    token = lax.broadcasted_iota(jnp.int32, (heads, tokens), 1)
    masked, visible = [], []
    peaks = jnp.full((heads, LANES), NEG_FLOOR, jnp.float32)
    for j in range(blocks):
        visible.append((token < seen[j]) & (token != targets[j]))
        value = jnp.where(visible[j], scores[j], NEG_FLOOR)
        masked.append(value)
        peaks = jnp.where(lane == j, jnp.max(value, axis=1, keepdims=True), peaks)
    group_peaks = jnp.zeros((heads, LANES), jnp.float32)
    sums = jnp.zeros((heads, LANES), jnp.float32)
    weights = []
    for j in range(blocks):
        same = owner_lanes == owners[j]
        peak = jnp.max(jnp.where(same, peaks, NEG_FLOOR), axis=1, keepdims=True)
        weights.append(
            jnp.where(visible[j], jnp.exp(masked[j] - peak), 0.0).astype(jnp.bfloat16)
        )
        weight = weights[j].astype(jnp.float32)
        group_peaks = jnp.where(lane == j, peak, group_peaks)
        sums = jnp.where(lane == j, jnp.sum(weight, axis=1, keepdims=True), sums)
    group_sums = jnp.zeros((heads, LANES), jnp.float32)
    leads = jnp.zeros((heads, LANES), jnp.float32)
    inverses = []
    for j in range(blocks):
        same = owner_lanes == owners[j]
        total = jnp.sum(jnp.where(same, sums, 0.0), axis=1, keepdims=True)
        group_sums = jnp.where(lane == j, total, group_sums)
        earlier = jnp.max(jnp.where(same & (lane < j), 1.0, 0.0), axis=1, keepdims=True)
        leads = jnp.where(lane == j, 1.0 - earlier, leads)
        inverses.append(jnp.where(total > 0.0, 1.0 / jnp.where(total > 0.0, total, 1.0), 0.0))
    quarter = LANES // 4
    stats = group_peaks
    for f, field in enumerate((group_sums, leads, owner_lanes.astype(jnp.float32))):
        stats = jnp.where(lane // quarter == f + 1, pltpu.roll(field, (f + 1) * quarter, 1), stats)
    table[core, first, second] = stats
    tables = Direct(table, (t0, t1, t2, t3), where)
    tables.start()
    lines = []
    for j in range(blocks):
        piece = jnp.dot(weights[j], cache[j, 1], preferred_element_type=jnp.float32)
        piece = jnp.where(head_mask, piece * inverses[j], 0.0)
        lines.append(jnp.sum(piece, axis=0, keepdims=True))
    for j in range(0, blocks, GROUP):
        pool[core, first, second, j : j + GROUP, :] = jnp.concatenate(
            lines[j : j + GROUP], axis=0
        ).astype(jnp.bfloat16)
    outputs = Gather(pool, (o0, o1, o2, o3, o4, o5), where, blocks)
    outputs.start()
    news.cross()
    outputs.relay()
    tables.cross((0, 1, 3, 2))
    news.finish()

    head_rows = jnp.where(head_mask, 1.0, 0.0).astype(jnp.bfloat16)
    product = query_pool[...].astype(jnp.float32) * fresh_pool[:, :, :, :, :columns].astype(
        jnp.float32
    )
    product = product.reshape(requests, columns)
    high = product.astype(jnp.bfloat16)
    low = (product - high.astype(jnp.float32)).astype(jnp.bfloat16)
    new_scores = sum(
        lax.dot_general(
            head_rows, piece, (((1,), (1,)), ((), ())), preferred_element_type=jnp.float32
        )
        for piece in (high, low)
    )
    tables.finish()

    devices = SIDE * SIDE
    split = devices * quarter
    request = lax.broadcasted_iota(jnp.int32, (requests, split), 0).astype(jnp.float32)

    def side(c):
        fields = [[] for _ in range(4)]
        for start in range(0, devices, 4):
            tiles = [table[c, d // SIDE, d % SIDE] for d in range(start, start + 4)]
            for f in range(4):
                merged = jnp.zeros((heads, LANES), jnp.float32)
                for k in range(4):
                    shift = (k - f) * quarter % LANES
                    tile = tiles[k] if shift == 0 else pltpu.roll(tiles[k], shift, 1)
                    merged = jnp.where(lane // quarter == k, tile, merged)
                fields[f].append(merged)
        fields = [jnp.concatenate(f, axis=1) for f in fields]
        used = lax.broadcasted_iota(jnp.int32, fields[3].shape, 1) % quarter < blocks
        fields[3] = jnp.where(used, fields[3], float(requests))
        is_long = jnp.zeros(fields[3].shape, jnp.bool_)
        for long_id in long_ids:
            is_long = is_long | (fields[3] == long_id)
        short_owner = jnp.where(is_long, float(requests), fields[3])[:1]
        member = jnp.where(request == short_owner, 1.0, 0.0).astype(jnp.bfloat16)
        led = jnp.concatenate(
            [thirds(jnp.where(fields[2] > 0.5, fields[f], 0.0)) for f in range(2)], axis=0
        ).astype(jnp.bfloat16)
        by_request = lax.dot_general(
            led, member, (((1,), (1,)), ((), ())), preferred_element_type=jnp.float32
        )
        return fields, member, by_request

    near_fields, near_member, by_request = side(core)
    far_fields, far_member, by_request_rest = side(1 - core)
    by_request = by_request + by_request_rest
    old_peak, old_mass = [
        by_request[i : i + heads]
        + by_request[i + heads : i + 2 * heads]
        + by_request[i + 2 * heads : i + 3 * heads]
        for i in (0, 3 * heads)
    ]
    request_lane = lax.broadcasted_iota(jnp.int32, (heads, requests), 1).astype(jnp.float32)
    peaks, sums, leads, slot_owners = [
        jnp.concatenate(pair, axis=1) for pair in zip(near_fields, far_fields)
    ]
    high_rows, low_rows = [], []
    for long_id in long_ids:
        match = slot_owners == long_id
        peak = jnp.max(jnp.where(match, peaks, NEG_FLOOR), axis=1, keepdims=True)
        mass = jnp.where(match, sums * jnp.exp(jnp.where(match, peaks, NEG_FLOOR) - peak), 0.0)
        whole_mass = jnp.sum(jnp.where(match, mass * leads, 0.0), axis=1, keepdims=True)
        weight = mass / whole_mass
        old_peak = jnp.where(request_lane == long_id, peak, old_peak)
        old_mass = jnp.where(request_lane == long_id, whole_mass, old_mass)
        high = weight.astype(jnp.bfloat16).astype(jnp.float32)
        high_rows.append(high)
        low_rows.append(weight - high)
    extra = jnp.concatenate(high_rows + low_rows, axis=0).astype(jnp.bfloat16)
    share = 1.0 / (1.0 + old_mass * jnp.exp(old_peak - new_scores))
    share = jnp.concatenate(
        [share, jnp.zeros((LANES - heads, requests), jnp.float32)], axis=0
    ).T
    head_tall = jnp.concatenate(
        [head_rows.astype(jnp.float32), jnp.zeros((LANES - heads, columns), jnp.float32)], axis=0
    ).astype(jnp.bfloat16)
    high = share.astype(jnp.bfloat16)
    low = (share - high.astype(jnp.float32)).astype(jnp.bfloat16)
    shares[...] = sum(
        jnp.dot(piece, head_tall, preferred_element_type=jnp.float32) for piece in (high, low)
    )
    row = lax.broadcasted_iota(jnp.int32, (requests, 1), 0).astype(jnp.float32)
    half = LONG_REQS * heads

    outputs.cross()
    values = pool[core].reshape(split, columns)
    old[...] = jnp.dot(near_member, values, preferred_element_type=jnp.float32)
    weighted = jnp.dot(extra[:, :split], values, preferred_element_type=jnp.float32)
    outputs.finish()
    values = pool[1 - core].reshape(split, columns)
    attended = old[...] + jnp.dot(far_member, values, preferred_element_type=jnp.float32)
    weighted = weighted + jnp.dot(extra[:, split:], values, preferred_element_type=jnp.float32)
    for l, long_id in enumerate(long_ids):
        both = weighted[l * heads : (l + 1) * heads] + weighted[
            half + l * heads : half + (l + 1) * heads
        ]
        line = jnp.sum(jnp.where(head_mask, both, 0.0), axis=0, keepdims=True)
        attended = jnp.where(row == long_id, line, attended)
    new_values = fresh_pool[:, :, :, :, columns:].astype(jnp.float32).reshape(requests, columns)
    attended = attended + shares[...] * (new_values - attended)
    result = lax.dot_general(
        attended.astype(jnp.bfloat16), w_out_ref[...], (((1,), (1,)), ((), ())),
        preferred_element_type=jnp.float32,
    )
    share = requests // SIDE
    result = result.reshape(SIDE, share, result.shape[1])
    exact[...] = result
    terms[...] = result.astype(jnp.bfloat16)
    copies = [
        send(terms.at[sides[i]], arrived.at[i], sem4s.at[i], sem4r.at[i], "tp", sides[i])
        for i in range(SIDE - 1)
    ]
    for part in range(2):
        at = slice(part * columns, (part + 1) * columns)
        rows_ref[:, at] = picked(fresh_pool[:, :, :, :, at]).astype(jnp.bfloat16)
    pairs = [
        states_ref[:, i * LANES : (i + 1) * LANES].astype(jnp.float32).T
        for i in range(requests // LANES)
    ]
    pair = jnp.where(tp // 2 == 0, pairs[0], pairs[1])
    total = exact[tp] + jnp.where(tp % 2 == 0, pair[:share], pair[share:])
    for copy in copies:
        copy.wait_recv()
    for i in range(SIDE - 1):
        total = total + arrived[i].astype(jnp.float32)
    hidden_ref[...] = total.astype(jnp.bfloat16)
    for group in (copies0, copies1, copies2):
        for copy in group.values():
            copy.wait_send()
    for gather in (queries, news, tables, outputs):
        gather.drain()
    for copy in copies:
        copy.wait_send()


def store_kernel(
    context_ref, owner_ref, index_ref, hidden_in_ref, rows_ref, cache_ref,
    hidden_ref, updated_ref, changed, sem,
):
    hidden_ref[...] = hidden_in_ref[...]
    blocks, _, tokens, columns = updated_ref.shape
    requests = context_ref.shape[0]
    groups = tokens // ROW_GROUP
    row = lax.broadcasted_iota(jnp.int32, (ROW_GROUP, columns), 0)
    for j in range(blocks):
        owner = owner_ref[j]
        last = context_ref[jnp.minimum(owner, requests - 1)] - 1
        hit = (owner < requests) & (index_ref[j] == last // tokens)
        place_in = last % tokens

        @pl.when(hit)
        def _(j=j, place_in=place_in):
            group = place_in // ROW_GROUP
            base = pl.multiple_of(group * ROW_GROUP, ROW_GROUP)
            for i in range(1, groups):
                at = pl.ds(pl.multiple_of((group + i) % groups * ROW_GROUP, ROW_GROUP), ROW_GROUP)
                pltpu.make_async_copy(
                    cache_ref.at[j, :, at], updated_ref.at[j, :, at], sem.at[j]
                ).start()
            for c in range(2):
                fresh = rows_ref[j : j + 1, c * columns : (c + 1) * columns]
                old = cache_ref[j, c, pl.ds(base, ROW_GROUP), :]
                changed[j, c] = jnp.where(
                    row == place_in - base, fresh.astype(jnp.float32), old.astype(jnp.float32)
                ).astype(jnp.bfloat16)
            pltpu.make_async_copy(
                changed.at[j], updated_ref.at[j, :, pl.ds(base, ROW_GROUP)], sem.at[j]
            ).start()

        @pl.when(jnp.logical_not(hit))
        def _(j=j):
            pltpu.make_async_copy(cache_ref.at[j], updated_ref.at[j], sem.at[j]).start()

    for j in range(blocks):
        pltpu.make_async_copy(cache_ref.at[j], updated_ref.at[j], sem.at[j]).wait()


def shards(states, norm_gain, w_qkv, w_out, cache, context_len, block_owner, block_index):
    requests, depth = states.shape
    parts, _, columns = w_qkv.shape
    width = parts * columns
    wide = width + LANES
    blocks = cache.shape[0]
    heads = columns // HEAD_DIM
    half_dim = HEAD_DIM // 2
    base = 10000.0 ** (-np.arange(half_dim, dtype=np.float64) * 2.0 / HEAD_DIM)
    frequency = jnp.asarray(np.tile(base, 2 * heads).astype(np.float32)[None, :])
    vmem = pl.BlockSpec(memory_space=pltpu.VMEM)
    smem = pl.BlockSpec(memory_space=pltpu.SMEM)
    hbm = pl.BlockSpec(memory_space=pltpu.HBM)
    dma = pltpu.SemaphoreType.DMA
    bf16 = jnp.bfloat16
    f32 = jnp.float32
    n = SIDE - 1
    share = requests // SIDE
    gather_sems = [dma((n,)), dma((n,)), dma((SIDE, n)), dma((SIDE, n)), dma((SIDE,)), dma((SIDE,))]
    hidden, rows = pl.pallas_call(
        step_kernel,
        name="step",
        out_shape=(
            jax.ShapeDtypeStruct((share, depth), bf16),
            jax.ShapeDtypeStruct((blocks, 2 * columns), bf16),
        ),
        in_specs=[hbm] * 10,
        out_specs=(vmem, vmem),
        scratch_shapes=[
            pltpu.SMEM((requests,), jnp.int32),
            pltpu.SMEM((blocks,), jnp.int32),
            pltpu.SMEM((blocks,), jnp.int32),
            pltpu.VMEM((2, requests // 2), jnp.int32),
            pltpu.VMEM((depth, requests), bf16),
            pltpu.VMEM((1, depth), bf16),
            pltpu.VMEM(w_qkv.shape, bf16),
            pltpu.VMEM((depth, columns), bf16),
            pltpu.VMEM((1, columns), f32),
            pltpu.VMEM(cache.shape, bf16),
            pltpu.VMEM((requests, depth), bf16),
            pltpu.VMEM((SIDE, SIDE, GROUP, wide), f32),
            pltpu.VMEM((SIDE, SIDE, GROUP, wide), bf16),
            pltpu.VMEM((SIDE, SIDE, GROUP, wide), bf16),
            pltpu.VMEM((n, SIDE, GROUP, wide), bf16),
            pltpu.VMEM((n, SIDE, GROUP, wide), bf16),
            pltpu.VMEM((n, GROUP, wide), bf16),
            pltpu.VMEM((n, GROUP, wide), bf16),
            pltpu.VMEM((2, SIDE, SIDE, GROUP, columns), bf16),
            pltpu.VMEM((2, SIDE, SIDE, GROUP, 2 * columns), bf16),
            pltpu.VMEM((blocks, columns), f32),
            pltpu.VMEM((blocks, heads, cache.shape[2]), f32),
            pltpu.VMEM((2, SIDE, SIDE, heads, LANES), f32),
            pltpu.VMEM((requests, columns), f32),
            pltpu.VMEM((requests, columns), f32),
            pltpu.VMEM((2, SIDE, SIDE, LANES // 4, columns), bf16),
            pltpu.VMEM((SIDE, share, depth), f32),
            pltpu.VMEM((SIDE, share, depth), bf16),
            pltpu.VMEM((n, share, depth), bf16),
            dma((10,)),
            dma((SIDE,)), dma((SIDE,)),
            dma((n, SIDE)), dma((n, SIDE)),
            dma((n,)), dma((n,)),
        ]
        + [dma((SIDE, SIDE)), dma((SIDE, SIDE)), dma((SIDE,)), dma((SIDE,))] * 2
        + gather_sems * 2
        + [dma((n,)), dma((n,))],
        compiler_params=pltpu.CompilerParams(
            collective_id=0, has_side_effects=True, vmem_limit_bytes=32 << 20
        ),
        cost_estimate=pl.CostEstimate(
            flops=10**9, bytes_accessed=cache.size * 2, transcendentals=10**5
        ),
    )(
        *(
            pltpu.with_memory_space_constraint(array, pltpu.HBM)
            for array in (
                context_len, block_owner, block_index, context_len.reshape(2, requests // 2),
                states.T, norm_gain[None, :], w_qkv, w_out.T, frequency, cache,
            )
        )
    )
    return pl.pallas_call(
        store_kernel,
        name="store",
        out_shape=(
            jax.ShapeDtypeStruct(hidden.shape, bf16),
            jax.ShapeDtypeStruct(cache.shape, bf16),
        ),
        in_specs=[smem, smem, smem, vmem, vmem, vmem],
        out_specs=(vmem, hbm),
        scratch_shapes=[pltpu.VMEM((blocks, 2, ROW_GROUP, columns), bf16), dma((blocks,))],
        compiler_params=pltpu.CompilerParams(vmem_limit_bytes=16 << 20),
    )(context_len, block_owner, block_index, hidden, rows, cache)


def solution(mesh):
    return jax.shard_map(
        shards,
        mesh=mesh,
        in_specs=(
            P(None, "seq"),
            P("seq"),
            P(None, "seq", "tp"),
            P("tp", "seq"),
            P("seq", None, None, "tp"),
            P(),
            P("seq"),
            P("seq"),
        ),
        out_specs=(P("tp", "seq"), P("seq", None, None, "tp")),
        check_vma=False,
    )
```

```python
import functools

import jax
import jax.numpy as jnp
import numpy as np
from jax import lax
from jax.experimental import pallas as pl
from jax.experimental.pallas import tpu as pltpu
from jax.sharding import PartitionSpec as P

HEAD_DIM = 96
EPSILON = 1e-05
NEG_FLOOR = -1e30
GROUP = 8
LANES = 128
SIDE = 4
LONG_LIMIT = 31 * 64
LONG_REQS = 4
ORDER = (2, 1, 3)
DEPARTURE = (1, 0, 2)
ARRIVAL = (0, 2, 1)
ROW_GROUP = 16


def place():
    me = lax.axis_index("seq")
    core = me % 2
    y = (me // 2) % SIDE
    z = me // (2 * SIDE)
    first = z * (1 - core) + y * core
    second = y * (1 - core) + z * core

    def device(a, b):
        zz = a * (1 - core) + b * core
        yy = b * (1 - core) + a * core
        return (zz * SIDE + yy) * 2 + core

    peers = {
        (i, j): device((first + i) % SIDE, (second + j) % SIDE)
        for i in range(SIDE)
        for j in range(SIDE)
        if (i, j) != (0, 0)
    }
    primary = [peers[i, 0] for i in range(1, SIDE)]
    secondary = [peers[0, j] for j in range(1, SIDE)]
    partner = me + 1 - 2 * core
    return core, first, second, partner, primary, secondary, peers


def send(src, dst, send_sem, recv_sem, axis, to):
    copy = pltpu.make_async_remote_copy(
        src_ref=src,
        dst_ref=dst,
        send_sem=send_sem,
        recv_sem=recv_sem,
        device_id={axis: to},
        device_id_type=pl.DeviceIdType.MESH,
    )
    copy.start()
    return copy


def greet(axis, others):
    barrier = pltpu.get_barrier_semaphore()
    for other in others:
        pl.semaphore_signal(
            barrier, inc=1, device_id={axis: other}, device_id_type=pl.DeviceIdType.MESH
        )


def halves(total):
    high = total.astype(jnp.bfloat16).astype(jnp.float32)
    lane = lax.broadcasted_iota(jnp.int32, total.shape, total.ndim - 1)
    return jnp.where(lane < LANES // 2, high, total - high).astype(jnp.bfloat16)


def whole(pair):
    pair = pair.astype(jnp.float32)
    return pair + pltpu.roll(pair, LANES // 2, pair.ndim - 1)


def rotated(values, cosine, sine, is_front):
    width = values.shape[-1]
    half = HEAD_DIM // 2
    other = jnp.where(
        is_front, pltpu.roll(values, width - half, 1), pltpu.roll(values, half, 1)
    )
    return values * cosine + other * sine


class Gather:
    def __init__(self, ref, sems, where, part=None):
        self.ref, self.part = ref, part
        self.core, self.first, self.second, self.partner, self.primary, self.secondary, _ = where
        self.near_s, self.near_r, self.far_s, self.far_r, self.swap_s, self.swap_r = sems
        self.far = {}
        self.swaps = []

    def view(self, *index):
        if self.part is None:
            return self.ref.at[index]
        fill = (slice(None),) * (3 - len(index))
        return self.ref.at[index + fill + (pl.ds(0, self.part),)]

    def forward(self, i, block):
        for k in DEPARTURE:
            self.far[i, k] = send(
                block, block, self.far_s.at[i, k], self.far_r.at[i, k], "seq", self.primary[k]
            )

    def start(self):
        block = self.view(self.core, self.first, self.second)
        self.near = {
            i: send(block, block, self.near_s.at[i], self.near_r.at[i], "seq", self.secondary[i])
            for i in DEPARTURE
        }
        self.forward(0, block)

    def relay(self):
        for i in ARRIVAL:
            self.near[i].wait_recv()
            self.forward(
                i + 1,
                self.view(self.core, self.first, (self.second + SIDE - 1 - i) % SIDE),
            )
        self.swap(0, self.view(self.core, self.first))

    def swap(self, k, group):
        self.swaps.append(
            send(group, group, self.swap_s.at[k], self.swap_r.at[k], "seq", self.partner)
        )

    def cross(self):
        for k in ARRIVAL:
            for i in range(SIDE):
                self.far[i, k].wait_recv()
            self.swap(k + 1, self.view(self.core, (self.first + SIDE - 1 - k) % SIDE))

    def finish(self):
        for copy in self.swaps:
            copy.wait_recv()

    def drain(self):
        for copy in list(self.near.values()) + list(self.far.values()) + self.swaps:
            copy.wait_send()


class Direct:
    def __init__(self, ref, sems, where):
        self.ref = ref
        self.core, self.first, _, self.partner, _, _, self.peers = where
        self.send_sem, self.recv_sem, self.swap_s, self.swap_r = sems
        self.second = where[2]
        self.swaps = []

    def start(self):
        block = self.ref.at[self.core, self.first, self.second]
        far = lambda at: min(at[0], SIDE - at[0]) + min(at[1], SIDE - at[1])
        self.copies = {
            at: send(
                block, block, self.send_sem.at[at], self.recv_sem.at[at], "seq", self.peers[at]
            )
            for at in sorted(self.peers, key=far, reverse=True)
        }

    def cross(self, groups):
        for i in groups:
            for j in range(SIDE):
                if (i, j) != (0, 0):
                    self.copies[i, j].wait_recv()
            group = self.ref.at[self.core, (self.first + SIDE - i) % SIDE]
            self.swaps.append(
                send(group, group, self.swap_s.at[i], self.swap_r.at[i], "seq", self.partner)
            )

    def finish(self):
        for copy in self.swaps:
            copy.wait_recv()

    def drain(self):
        for copy in list(self.copies.values()) + self.swaps:
            copy.wait_send()


def thirds(value):
    pieces = []
    for _ in range(3):
        piece = value.astype(jnp.bfloat16).astype(jnp.float32)
        pieces.append(piece)
        value = value - piece
    return jnp.concatenate(pieces, axis=0)


def step_kernel(
    context_hbm, owner_hbm, index_hbm, lens_hbm, states_hbm, gain_hbm, w_hbm, w_out_hbm,
    frequency_hbm, cache_hbm,
    hidden_ref, rows_ref,
    context_ref, owner_ref, index_ref, lens_ref, states_ref, gain_ref, w_ref, w_out_ref,
    frequency_ref, cache, scaled, own, snd0, rcv0, snd1, rcv1, snd2, rcv2, query_pool, fresh_pool, query_rows,
    scores, table, shares, old, pool, exact, terms, arrived,
    sem_in, sem0s, sem0r, sem1s, sem1r, sem2s, sem2r,
    q0, q1, q2, q3, t0, t1, t2, t3, k0, k1, k2, k3, k4, k5, o0, o1, o2, o3, o4, o5, sem4s, sem4r,
):
    where = place()
    core, first, second, partner, primary, secondary, peers = where
    tp = lax.axis_index("tp")
    sides = [(tp + i) % SIDE for i in range(1, SIDE)]
    greet("seq", [partner] + primary + secondary)
    greet("tp", sides)
    loads = {}
    for i, (name, source, target) in enumerate(
        (
            ("states", states_hbm, states_ref), ("gain", gain_hbm, gain_ref),
            ("w", w_hbm, w_ref), ("context", context_hbm, context_ref),
            ("owner", owner_hbm, owner_ref), ("index", index_hbm, index_ref),
            ("lens", lens_hbm, lens_ref), ("frequency", frequency_hbm, frequency_ref),
            ("w_out", w_out_hbm, w_out_ref), ("cache", cache_hbm, cache),
        )
    ):
        loads[name] = pltpu.make_async_copy(source, target, sem_in.at[i])
        loads[name].start()

    parts, _, columns = w_ref.shape
    width = parts * columns
    blocks, _, tokens, _ = cache.shape
    heads = columns // HEAD_DIM
    requests = context_ref.shape[0]
    half_rows = requests // 2

    loads["states"].wait()
    loads["gain"].wait()
    states = states_ref[...].astype(jnp.float32).T
    scaled[...] = (states * gain_ref[...].astype(jnp.float32)).astype(jnp.bfloat16)
    squares = jnp.sum(states * states, axis=1, keepdims=True)
    squares = jnp.broadcast_to(squares, (requests, LANES))
    squares = [squares[:half_rows], squares[half_rows:]]
    shape = (SIDE, SIDE, GROUP)
    loads["w"].wait()
    rows = scaled[pl.ds(pl.multiple_of((1 - core) * half_rows, half_rows), half_rows), :]
    for part in range(parts):
        term = jnp.dot(rows, w_ref[part], preferred_element_type=jnp.float32)
        snd0[:, :, :, part * columns : (part + 1) * columns] = term.reshape(
            shape + (columns,)
        ).astype(jnp.bfloat16)
    snd0[:, :, :, width:] = halves(jnp.where(core == 0, squares[1], squares[0])).reshape(
        shape + (LANES,)
    )
    pl.semaphore_wait(pltpu.get_barrier_semaphore(), 10)
    copies0 = {}
    for i in ORDER + (0,):
        b = (first + i) % SIDE
        copies0[i] = send(
            snd0.at[:, b], rcv0.at[:, b], sem0s.at[i], sem0r.at[i], "seq", partner
        )
    rows = scaled[pl.ds(pl.multiple_of(core * half_rows, half_rows), half_rows), :]
    for part in range(parts):
        term = jnp.dot(rows, w_ref[part], preferred_element_type=jnp.float32)
        own[:, :, :, part * columns : (part + 1) * columns] = term.reshape(shape + (columns,))
    own[:, :, :, width:] = jnp.where(core == 0, squares[0], squares[1]).reshape(shape + (LANES,))

    copies1 = {}
    for j in ORDER + (0,):
        copies0[j].wait_recv()
        b = (second + j) % SIDE
        for i in ORDER:
            a = (first + i) % SIDE
            snd1[i - 1, j, :, :width] = (
                own[a, b, :, :width] + rcv0[a, b, :, :width].astype(jnp.float32)
            ).astype(jnp.bfloat16)
            snd1[i - 1, j, :, width:] = halves(own[a, b, :, width:] + whole(rcv0[a, b, :, width:]))
            copies1[i, j] = send(
                snd1.at[i - 1, j], rcv1.at[i - 1, j], sem1s.at[i - 1, j], sem1r.at[i - 1, j],
                "seq", primary[i - 1],
            )

    for name in ("context", "owner", "index", "lens", "frequency", "w_out"):
        loads[name].wait()
    here = (core * SIDE + first) * SIDE + second
    row = lax.broadcasted_iota(jnp.int32, (GROUP, columns), 0)
    position = jnp.zeros((GROUP, columns), jnp.int32)
    for i in range(GROUP):
        position = jnp.where(row == i, context_ref[here * GROUP + i] - 1, position)
    angle = position.astype(jnp.float32) * frequency_ref[...]
    cosine = jnp.cos(angle)
    is_front = lax.broadcasted_iota(jnp.int32, (GROUP, columns), 1) % HEAD_DIM < HEAD_DIM // 2
    sine = jnp.sin(angle)
    sine = jnp.where(is_front, -sine, sine)

    copies2 = {}
    for j in ORDER + (0,):
        b = (second + j) % SIDE
        term = own[first, b, :, :width] + rcv0[first, b, :, :width].astype(jnp.float32)
        total = own[first, b, :, width:] + whole(rcv0[first, b, :, width:])
        for i in ORDER:
            copies1[i, j].wait_recv()
            term = term + rcv1[i - 1, j, :, :width].astype(jnp.float32)
            total = total + whole(rcv1[i - 1, j, :, width:])
        if j:
            snd2[j - 1, :, :width] = term.astype(jnp.bfloat16)
            snd2[j - 1, :, width:] = halves(total)
            copies2[j] = send(
                snd2.at[j - 1], rcv2.at[j - 1], sem2s.at[j - 1], sem2r.at[j - 1],
                "seq", secondary[j - 1],
            )
    slot = lax.broadcasted_iota(jnp.int32, (blocks, requests), 0)
    wanted = jnp.zeros((blocks, requests), jnp.int32)
    lane = lax.broadcasted_iota(jnp.int32, (heads, LANES), 1)
    owner_lanes = jnp.full((heads, LANES), requests, jnp.int32)
    owners, seen, targets = [], [], []
    for j in range(blocks):
        owner = owner_ref[j]
        live = owner < requests
        last = context_ref[jnp.minimum(owner, requests - 1)] - 1
        hit = live & (index_ref[j] == last // tokens)
        wanted = jnp.where(slot == j, owner, wanted)
        owner_lanes = jnp.where(lane == j, owner, owner_lanes)
        owners.append(owner)
        seen.append(jnp.where(live, last + 1 - index_ref[j] * tokens, 0))
        targets.append(jnp.where(hit, last % tokens, -1))
    pick = jnp.where(
        lax.broadcasted_iota(jnp.int32, (blocks, requests), 1) == wanted, 1.0, 0.0
    ).astype(jnp.bfloat16)
    head_mask = (
        lax.broadcasted_iota(jnp.int32, (heads, columns), 1) // HEAD_DIM
        == lax.broadcasted_iota(jnp.int32, (heads, columns), 0)
    )
    pool[:, :, :, blocks:, :] = jnp.zeros(
        (2, SIDE, SIDE, pool.shape[3] - blocks, pool.shape[4]), jnp.bfloat16
    )
    lens = lens_ref[...]
    ids = lax.broadcasted_iota(jnp.int32, lens.shape, 0) * lens.shape[1] + (
        lax.broadcasted_iota(jnp.int32, lens.shape, 1)
    )
    candidates = jnp.where(lens > LONG_LIMIT, ids, -1).astype(jnp.float32)
    long_ids = []
    for _ in range(LONG_REQS):
        top = jnp.max(jnp.max(candidates, axis=1, keepdims=True), axis=0, keepdims=True)
        long_ids.append(top)
        candidates = jnp.where(candidates == top, -1.0, candidates)
    loads["cache"].wait()
    for j in (1, 3, 2):
        copies2[j].wait_recv()
        term = term + rcv2[j - 1, :, :width].astype(jnp.float32)
        total = total + whole(rcv2[j - 1, :, width:])

    inverse = lax.rsqrt(total / (HEAD_DIM * 32) + EPSILON)[:, :1]
    query = rotated(term[:, :columns] * inverse, cosine, sine, is_front) * HEAD_DIM ** (-0.5)
    query_pool[core, first, second] = query.astype(jnp.bfloat16)
    queries = Direct(query_pool, (q0, q1, q2, q3), where)
    queries.start()
    key = rotated(term[:, columns : 2 * columns] * inverse, cosine, sine, is_front)
    fresh_pool[core, first, second, :, :columns] = key.astype(jnp.bfloat16)
    fresh_pool[core, first, second, :, columns:] = (term[:, 2 * columns :] * inverse).astype(
        jnp.bfloat16
    )
    news = Gather(fresh_pool, (k0, k1, k2, k3, k4, k5), where)
    news.start()
    queries.cross((0,))
    news.relay()
    queries.cross((1, 3, 2))
    queries.finish()

    def picked(piece):
        piece = piece.astype(jnp.float32).reshape(requests, columns).astype(jnp.bfloat16)
        return jnp.dot(pick, piece, preferred_element_type=jnp.float32)

    query_rows[...] = picked(query_pool[...])
    for j in range(blocks):
        spread = jnp.where(head_mask, query_rows[j : j + 1, :], 0.0).astype(jnp.bfloat16)
        scores[j] = lax.dot_general(
            spread, cache[j, 0], (((1,), (1,)), ((), ())), preferred_element_type=jnp.float32
        )

    token = lax.broadcasted_iota(jnp.int32, (heads, tokens), 1)
    masked, visible = [], []
    peaks = jnp.full((heads, LANES), NEG_FLOOR, jnp.float32)
    for j in range(blocks):
        visible.append((token < seen[j]) & (token != targets[j]))
        value = jnp.where(visible[j], scores[j], NEG_FLOOR)
        masked.append(value)
        peaks = jnp.where(lane == j, jnp.max(value, axis=1, keepdims=True), peaks)
    group_peaks = jnp.zeros((heads, LANES), jnp.float32)
    sums = jnp.zeros((heads, LANES), jnp.float32)
    weights = []
    for j in range(blocks):
        same = owner_lanes == owners[j]
        peak = jnp.max(jnp.where(same, peaks, NEG_FLOOR), axis=1, keepdims=True)
        weights.append(
            jnp.where(visible[j], jnp.exp(masked[j] - peak), 0.0).astype(jnp.bfloat16)
        )
        weight = weights[j].astype(jnp.float32)
        group_peaks = jnp.where(lane == j, peak, group_peaks)
        sums = jnp.where(lane == j, jnp.sum(weight, axis=1, keepdims=True), sums)
    group_sums = jnp.zeros((heads, LANES), jnp.float32)
    leads = jnp.zeros((heads, LANES), jnp.float32)
    inverses = []
    for j in range(blocks):
        same = owner_lanes == owners[j]
        total = jnp.sum(jnp.where(same, sums, 0.0), axis=1, keepdims=True)
        group_sums = jnp.where(lane == j, total, group_sums)
        earlier = jnp.max(jnp.where(same & (lane < j), 1.0, 0.0), axis=1, keepdims=True)
        leads = jnp.where(lane == j, 1.0 - earlier, leads)
        inverses.append(jnp.where(total > 0.0, 1.0 / jnp.where(total > 0.0, total, 1.0), 0.0))
    quarter = LANES // 4
    stats = group_peaks
    for f, field in enumerate((group_sums, leads, owner_lanes.astype(jnp.float32))):
        stats = jnp.where(lane // quarter == f + 1, pltpu.roll(field, (f + 1) * quarter, 1), stats)
    table[core, first, second] = stats
    tables = Direct(table, (t0, t1, t2, t3), where)
    tables.start()
    lines = []
    for j in range(blocks):
        piece = jnp.dot(weights[j], cache[j, 1], preferred_element_type=jnp.float32)
        piece = jnp.where(head_mask, piece * inverses[j], 0.0)
        lines.append(jnp.sum(piece, axis=0, keepdims=True))
    for j in range(0, blocks, GROUP):
        pool[core, first, second, j : j + GROUP, :] = jnp.concatenate(
            lines[j : j + GROUP], axis=0
        ).astype(jnp.bfloat16)
    outputs = Gather(pool, (o0, o1, o2, o3, o4, o5), where, blocks)
    outputs.start()
    news.cross()
    outputs.relay()
    tables.cross((0, 1, 3, 2))

    tables.finish()

    devices = SIDE * SIDE
    split = devices * quarter
    request = lax.broadcasted_iota(jnp.int32, (requests, split), 0).astype(jnp.float32)

    def side(c):
        fields = [[] for _ in range(4)]
        for start in range(0, devices, 4):
            tiles = [table[c, d // SIDE, d % SIDE] for d in range(start, start + 4)]
            for f in range(4):
                merged = jnp.zeros((heads, LANES), jnp.float32)
                for k in range(4):
                    shift = (k - f) * quarter % LANES
                    tile = tiles[k] if shift == 0 else pltpu.roll(tiles[k], shift, 1)
                    merged = jnp.where(lane // quarter == k, tile, merged)
                fields[f].append(merged)
        fields = [jnp.concatenate(f, axis=1) for f in fields]
        used = lax.broadcasted_iota(jnp.int32, fields[3].shape, 1) % quarter < blocks
        fields[3] = jnp.where(used, fields[3], float(requests))
        is_long = jnp.zeros(fields[3].shape, jnp.bool_)
        for long_id in long_ids:
            is_long = is_long | (fields[3] == long_id)
        short_owner = jnp.where(is_long, float(requests), fields[3])[:1]
        member = jnp.where(request == short_owner, 1.0, 0.0).astype(jnp.bfloat16)
        led = jnp.concatenate(
            [thirds(jnp.where(fields[2] > 0.5, fields[f], 0.0)) for f in range(2)], axis=0
        ).astype(jnp.bfloat16)
        by_request = lax.dot_general(
            led, member, (((1,), (1,)), ((), ())), preferred_element_type=jnp.float32
        )
        return fields, member, by_request

    near_fields, near_member, by_request = side(core)
    far_fields, far_member, by_request_rest = side(1 - core)
    by_request = by_request + by_request_rest
    old_peak, old_mass = [
        by_request[i : i + heads]
        + by_request[i + heads : i + 2 * heads]
        + by_request[i + 2 * heads : i + 3 * heads]
        for i in (0, 3 * heads)
    ]
    request_lane = lax.broadcasted_iota(jnp.int32, (heads, requests), 1).astype(jnp.float32)
    peaks, sums, leads, slot_owners = [
        jnp.concatenate(pair, axis=1) for pair in zip(near_fields, far_fields)
    ]
    high_rows, low_rows = [], []
    for long_id in long_ids:
        match = slot_owners == long_id
        peak = jnp.max(jnp.where(match, peaks, NEG_FLOOR), axis=1, keepdims=True)
        mass = jnp.where(match, sums * jnp.exp(jnp.where(match, peaks, NEG_FLOOR) - peak), 0.0)
        whole_mass = jnp.sum(jnp.where(match, mass * leads, 0.0), axis=1, keepdims=True)
        weight = mass / whole_mass
        old_peak = jnp.where(request_lane == long_id, peak, old_peak)
        old_mass = jnp.where(request_lane == long_id, whole_mass, old_mass)
        high = weight.astype(jnp.bfloat16).astype(jnp.float32)
        high_rows.append(high)
        low_rows.append(weight - high)
    extra = jnp.concatenate(high_rows + low_rows, axis=0).astype(jnp.bfloat16)
    outputs.cross()
    news.finish()
    head_rows = jnp.where(head_mask, 1.0, 0.0).astype(jnp.bfloat16)
    product = query_pool[...].astype(jnp.float32) * fresh_pool[:, :, :, :, :columns].astype(
        jnp.float32
    )
    product = product.reshape(requests, columns)
    high = product.astype(jnp.bfloat16)
    low = (product - high.astype(jnp.float32)).astype(jnp.bfloat16)
    new_scores = sum(
        lax.dot_general(
            head_rows, piece, (((1,), (1,)), ((), ())), preferred_element_type=jnp.float32
        )
        for piece in (high, low)
    )
    share = 1.0 / (1.0 + old_mass * jnp.exp(old_peak - new_scores))
    share = jnp.concatenate(
        [share, jnp.zeros((LANES - heads, requests), jnp.float32)], axis=0
    ).T
    head_tall = jnp.concatenate(
        [head_rows.astype(jnp.float32), jnp.zeros((LANES - heads, columns), jnp.float32)], axis=0
    ).astype(jnp.bfloat16)
    high = share.astype(jnp.bfloat16)
    low = (share - high.astype(jnp.float32)).astype(jnp.bfloat16)
    shares[...] = sum(
        jnp.dot(piece, head_tall, preferred_element_type=jnp.float32) for piece in (high, low)
    )
    row = lax.broadcasted_iota(jnp.int32, (requests, 1), 0).astype(jnp.float32)
    half = LONG_REQS * heads

    values = pool[core].reshape(split, columns)
    old[...] = jnp.dot(near_member, values, preferred_element_type=jnp.float32)
    weighted = jnp.dot(extra[:, :split], values, preferred_element_type=jnp.float32)
    outputs.finish()
    values = pool[1 - core].reshape(split, columns)
    attended = old[...] + jnp.dot(far_member, values, preferred_element_type=jnp.float32)
    weighted = weighted + jnp.dot(extra[:, split:], values, preferred_element_type=jnp.float32)
    for l, long_id in enumerate(long_ids):
        both = weighted[l * heads : (l + 1) * heads] + weighted[
            half + l * heads : half + (l + 1) * heads
        ]
        line = jnp.sum(jnp.where(head_mask, both, 0.0), axis=0, keepdims=True)
        attended = jnp.where(row == long_id, line, attended)
    new_values = fresh_pool[:, :, :, :, columns:].astype(jnp.float32).reshape(requests, columns)
    attended = attended + shares[...] * (new_values - attended)
    result = lax.dot_general(
        attended.astype(jnp.bfloat16), w_out_ref[...], (((1,), (1,)), ((), ())),
        preferred_element_type=jnp.float32,
    )
    share = requests // SIDE
    result = result.reshape(SIDE, share, result.shape[1])
    exact[...] = result
    terms[...] = result.astype(jnp.bfloat16)
    copies = [
        send(terms.at[sides[i]], arrived.at[i], sem4s.at[i], sem4r.at[i], "tp", sides[i])
        for i in range(SIDE - 1)
    ]
    for part in range(2):
        at = slice(part * columns, (part + 1) * columns)
        rows_ref[:, at] = picked(fresh_pool[:, :, :, :, at]).astype(jnp.bfloat16)
    pairs = [
        states_ref[:, i * LANES : (i + 1) * LANES].astype(jnp.float32).T
        for i in range(requests // LANES)
    ]
    pair = jnp.where(tp // 2 == 0, pairs[0], pairs[1])
    total = exact[tp] + jnp.where(tp % 2 == 0, pair[:share], pair[share:])
    for copy in copies:
        copy.wait_recv()
    for i in range(SIDE - 1):
        total = total + arrived[i].astype(jnp.float32)
    hidden_ref[...] = total.astype(jnp.bfloat16)
    for group in (copies0, copies1, copies2):
        for copy in group.values():
            copy.wait_send()
    for gather in (queries, news, tables, outputs):
        gather.drain()
    for copy in copies:
        copy.wait_send()


def store_kernel(
    context_ref, owner_ref, index_ref, hidden_in_ref, rows_ref, cache_ref,
    hidden_ref, updated_ref, changed, sem,
):
    hidden_ref[...] = hidden_in_ref[...]
    blocks, _, tokens, columns = updated_ref.shape
    requests = context_ref.shape[0]
    groups = tokens // ROW_GROUP
    row = lax.broadcasted_iota(jnp.int32, (ROW_GROUP, columns), 0)
    for j in range(blocks):
        owner = owner_ref[j]
        last = context_ref[jnp.minimum(owner, requests - 1)] - 1
        hit = (owner < requests) & (index_ref[j] == last // tokens)
        place_in = last % tokens

        @pl.when(hit)
        def _(j=j, place_in=place_in):
            group = place_in // ROW_GROUP
            base = pl.multiple_of(group * ROW_GROUP, ROW_GROUP)
            for i in range(1, groups):
                at = pl.ds(pl.multiple_of((group + i) % groups * ROW_GROUP, ROW_GROUP), ROW_GROUP)
                pltpu.make_async_copy(
                    cache_ref.at[j, :, at], updated_ref.at[j, :, at], sem.at[j]
                ).start()
            for c in range(2):
                fresh = rows_ref[j : j + 1, c * columns : (c + 1) * columns]
                old = cache_ref[j, c, pl.ds(base, ROW_GROUP), :]
                changed[j, c] = jnp.where(
                    row == place_in - base, fresh.astype(jnp.float32), old.astype(jnp.float32)
                ).astype(jnp.bfloat16)
            pltpu.make_async_copy(
                changed.at[j], updated_ref.at[j, :, pl.ds(base, ROW_GROUP)], sem.at[j]
            ).start()

        @pl.when(jnp.logical_not(hit))
        def _(j=j):
            pltpu.make_async_copy(cache_ref.at[j], updated_ref.at[j], sem.at[j]).start()

    for j in range(blocks):
        pltpu.make_async_copy(cache_ref.at[j], updated_ref.at[j], sem.at[j]).wait()


def shards(states, norm_gain, w_qkv, w_out, cache, context_len, block_owner, block_index):
    requests, depth = states.shape
    parts, _, columns = w_qkv.shape
    width = parts * columns
    wide = width + LANES
    blocks = cache.shape[0]
    heads = columns // HEAD_DIM
    half_dim = HEAD_DIM // 2
    base = 10000.0 ** (-np.arange(half_dim, dtype=np.float64) * 2.0 / HEAD_DIM)
    frequency = jnp.asarray(np.tile(base, 2 * heads).astype(np.float32)[None, :])
    vmem = pl.BlockSpec(memory_space=pltpu.VMEM)
    smem = pl.BlockSpec(memory_space=pltpu.SMEM)
    hbm = pl.BlockSpec(memory_space=pltpu.HBM)
    dma = pltpu.SemaphoreType.DMA
    bf16 = jnp.bfloat16
    f32 = jnp.float32
    n = SIDE - 1
    share = requests // SIDE
    gather_sems = [dma((n,)), dma((n,)), dma((SIDE, n)), dma((SIDE, n)), dma((SIDE,)), dma((SIDE,))]
    hidden, rows = pl.pallas_call(
        step_kernel,
        name="step",
        out_shape=(
            jax.ShapeDtypeStruct((share, depth), bf16),
            jax.ShapeDtypeStruct((blocks, 2 * columns), bf16),
        ),
        in_specs=[hbm] * 10,
        out_specs=(vmem, vmem),
        scratch_shapes=[
            pltpu.SMEM((requests,), jnp.int32),
            pltpu.SMEM((blocks,), jnp.int32),
            pltpu.SMEM((blocks,), jnp.int32),
            pltpu.VMEM((2, requests // 2), jnp.int32),
            pltpu.VMEM((depth, requests), bf16),
            pltpu.VMEM((1, depth), bf16),
            pltpu.VMEM(w_qkv.shape, bf16),
            pltpu.VMEM((depth, columns), bf16),
            pltpu.VMEM((1, columns), f32),
            pltpu.VMEM(cache.shape, bf16),
            pltpu.VMEM((requests, depth), bf16),
            pltpu.VMEM((SIDE, SIDE, GROUP, wide), f32),
            pltpu.VMEM((SIDE, SIDE, GROUP, wide), bf16),
            pltpu.VMEM((SIDE, SIDE, GROUP, wide), bf16),
            pltpu.VMEM((n, SIDE, GROUP, wide), bf16),
            pltpu.VMEM((n, SIDE, GROUP, wide), bf16),
            pltpu.VMEM((n, GROUP, wide), bf16),
            pltpu.VMEM((n, GROUP, wide), bf16),
            pltpu.VMEM((2, SIDE, SIDE, GROUP, columns), bf16),
            pltpu.VMEM((2, SIDE, SIDE, GROUP, 2 * columns), bf16),
            pltpu.VMEM((blocks, columns), f32),
            pltpu.VMEM((blocks, heads, cache.shape[2]), f32),
            pltpu.VMEM((2, SIDE, SIDE, heads, LANES), f32),
            pltpu.VMEM((requests, columns), f32),
            pltpu.VMEM((requests, columns), f32),
            pltpu.VMEM((2, SIDE, SIDE, LANES // 4, columns), bf16),
            pltpu.VMEM((SIDE, share, depth), f32),
            pltpu.VMEM((SIDE, share, depth), bf16),
            pltpu.VMEM((n, share, depth), bf16),
            dma((10,)),
            dma((SIDE,)), dma((SIDE,)),
            dma((n, SIDE)), dma((n, SIDE)),
            dma((n,)), dma((n,)),
        ]
        + [dma((SIDE, SIDE)), dma((SIDE, SIDE)), dma((SIDE,)), dma((SIDE,))] * 2
        + gather_sems * 2
        + [dma((n,)), dma((n,))],
        compiler_params=pltpu.CompilerParams(
            collective_id=0, has_side_effects=True, vmem_limit_bytes=32 << 20
        ),
        cost_estimate=pl.CostEstimate(
            flops=10**9, bytes_accessed=cache.size * 2, transcendentals=10**5
        ),
    )(
        *(
            pltpu.with_memory_space_constraint(array, pltpu.HBM)
            for array in (
                context_len, block_owner, block_index, context_len.reshape(2, requests // 2),
                states.T, norm_gain[None, :], w_qkv, w_out.T, frequency, cache,
            )
        )
    )
    return pl.pallas_call(
        store_kernel,
        name="store",
        out_shape=(
            jax.ShapeDtypeStruct(hidden.shape, bf16),
            jax.ShapeDtypeStruct(cache.shape, bf16),
        ),
        in_specs=[smem, smem, smem, vmem, vmem, vmem],
        out_specs=(vmem, hbm),
        scratch_shapes=[pltpu.VMEM((blocks, 2, ROW_GROUP, columns), bf16), dma((blocks,))],
        compiler_params=pltpu.CompilerParams(vmem_limit_bytes=16 << 20),
    )(context_len, block_owner, block_index, hidden, rows, cache)


def solution(mesh):
    return jax.shard_map(
        shards,
        mesh=mesh,
        in_specs=(
            P(None, "seq"),
            P("seq"),
            P(None, "seq", "tp"),
            P("tp", "seq"),
            P("seq", None, None, "tp"),
            P(),
            P("seq"),
            P("seq"),
        ),
        out_specs=(P("tp", "seq"), P("seq", None, None, "tp")),
        check_vma=False,
    )
```
